512 devices in a mesh: ep: 16 (over z_hi, y), sp: 32 (over z_lo, x, core).
Axes of the slice: x: 4, y: 8, z: 8 (z_hi: 2, z_lo: 4; z = z_hi * 4 + z_lo), core: 2. Of those that a mesh axis runs over, the one named last changes fastest.
Arguments:
- grad_out: bfloat16 [65536, 4096], P(('ep', 'sp')), may hold values from -1.5 to 1.5
- routes: int32 [65536, 8], P(('ep', 'sp')), may hold values from 0 to 127, as said below
- gate: bfloat16 [65536, 8], P(('ep', 'sp')), may hold values from 0.049804688 to 1
- saved: bfloat16 [16, 32, 256, 3072], P('ep', 'sp'), may hold values from -6 to 6
- w_down: bfloat16 [16, 1536, 4096], P('ep', None, 'sp'), may hold values from -0.15625 to 0.15625
Outputs:
- grad_pre: bfloat16 [16, 32, 256, 3072], P('ep', 'sp')
- grad_gate: float32 [65536, 8], P(('ep', 'sp'))
The draws below stay inside these ranges and needn't reach their ends.
Inputs may be any that keep to these rules, and one draw needn't show every extreme that they name: `routes`: each row names 8 different experts. In every block of 128 rows at most 16 rows name the same expert whose number is a multiple of 8, and in every block one such expert is named by exactly 16 rows; it is the same expert for all blocks whose indices agree modulo 32.
All inputs are finite; a program needn't handle non-finite values.
Results may differ from the reference program's by a relative error of at most 0.0029.
Values may be sent and summed in bfloat16 or wider, within the bound.
No kernel may reach another device: no remote copies, remote signals or barrier semaphores. Data moves between devices by JAX's collectives and lax.ppermute only.
A program may use at most 128 MiB of HBM per device.

```python
import jax
import jax.numpy as jnp
from jax import lax

D = 4096
FF = 1536
EXPERTS = 128
TOP = 8
TOK_DEV = 128
CAP = 16
EXP_DEV = 8
WAVE = 16
SPLITS = 32
TOKENS = 65536


def draw_routes(key, part):
    flights = EXPERTS // EXP_DEV
    blocks = TOKENS // TOK_DEV
    split_count = blocks // flights
    subkeys = jax.random.split(jax.random.fold_in(key, 17), 5)
    heat_level = jax.random.randint(subkeys[0], (flights,), 0, 4)
    base_count = jax.random.randint(subkeys[1], (blocks, flights), 0, CAP // 2 + 1)
    counts = jnp.minimum(base_count * (heat_level[None, :] + 1), CAP)
    chosen = jax.random.randint(subkeys[2], (split_count,), 0, flights)
    forced = jnp.tile(chosen, blocks // split_count)
    is_forced = jnp.arange(flights)[None, :] == forced[:, None]
    counts = jnp.where(is_forced, CAP, counts)
    rank_raw = jax.random.randint(subkeys[3], (blocks, flights, TOK_DEV), 0, 1 << 16) * TOK_DEV + jnp.arange(TOK_DEV)[None, None, :]
    ordering = jnp.argsort(rank_raw, axis=2)
    rank_of = jnp.argsort(ordering, axis=2)
    picked = rank_of < counts[:, :, None]
    member = jnp.transpose(picked, (0, 2, 1)).reshape(TOKENS, flights)
    forced_tok = jnp.transpose(picked & is_forced[:, :, None], (0, 2, 1)).reshape(TOKENS, flights)
    expert_numbers = jnp.arange(EXPERTS)
    score_values = jax.random.randint(subkeys[4], (TOKENS, EXPERTS), 0, 1 << 16) * EXPERTS + expert_numbers[None, :]
    in_wave = expert_numbers % EXP_DEV == 0
    wave_of = expert_numbers // EXP_DEV
    membership_per_expert = jnp.take(member, wave_of, axis=1)
    compelled_per_expert = jnp.take(forced_tok, wave_of, axis=1).astype(jnp.int32)
    extra_length = 1 << 24
    wave_routing_scores = jnp.where(membership_per_expert, extra_length + compelled_per_expert * extra_length + score_values, -1 - expert_numbers[None, :])
    score_values = jnp.where(in_wave[None, :], wave_routing_scores, score_values)
    top_values, routes = lax.top_k(score_values, TOP)
    return routes.astype(jnp.int32)


def shard_levels(stream_key, shape, cuts, smallest, top_value):
    def one(axis_at, blocks):
        steps = jax.random.uniform(jax.random.fold_in(jax.random.fold_in(stream_key, 6), axis_at), (blocks,), jnp.float32, smallest / len(cuts), top_value / len(cuts))
        return jnp.repeat(jnp.exp(steps), shape[axis_at] // blocks).reshape((-1,) + (1,) * (len(shape) - axis_at - 1))

    level = one(*cuts[0])
    for cut in cuts[1:]:
        level = level * one(*cut)
    return level


def noise(own_key, extent, width, most, shards=(), kind=jnp.bfloat16):
    drawn = width * jax.random.normal(own_key, extent, jnp.float32)
    if shards:
        drawn = drawn * shard_levels(own_key, extent, shards, -0.22, 0.18)
    return jnp.clip(drawn, -most, most).astype(kind)


def setup_inputs(seed: int = 0) -> dict:
    key_list = jax.random.split(jax.random.key(seed), 6)
    grad_out = noise(key_list[0], (TOKENS, D), 0.25, 1.5, ((0, 512),))
    routes = draw_routes(jax.random.fold_in(key_list[5], 71), 0)
    gate = jnp.clip(0.049804688 + 0.9501953 * jax.random.uniform(key_list[2], (TOKENS, TOP), jnp.float32) ** shard_levels(key_list[2], (TOKENS, TOP), ((0, 512),), -0.2, 0.2), 0.049804688, 1.0).astype(jnp.bfloat16)
    saved = noise(key_list[3], (WAVE, SPLITS, WAVE * CAP, 2 * FF), 1.0, 6.0, ((0, 16), (1, 32)))
    w_down = noise(key_list[4], (WAVE, FF, D), FF ** -0.5, 0.15625, ((0, 16), (2, 32)))
    return dict(grad_out=grad_out, routes=routes, gate=gate, saved=saved, w_down=w_down)


def reference(grad_out, routes, gate, saved, w_down):
    flight = (routes % EXP_DEV) == 0
    owners = (routes // EXP_DEV).astype(jnp.int32)
    wave_ids = jnp.arange(WAVE, dtype=jnp.int32)
    onehot = (owners[:, :, None] == wave_ids[None, None, :]) & flight[:, :, None]
    member = jnp.sum(onehot.astype(jnp.int32), axis=1)
    gate_by_expert = jnp.sum(onehot.astype(jnp.float32) * gate.astype(jnp.float32)[:, :, None], axis=1)
    blocked_rows = member.reshape(TOKENS // TOK_DEV, TOK_DEV, WAVE)
    places = (jnp.cumsum(blocked_rows, axis=1) - blocked_rows).reshape(TOKENS, WAVE).astype(jnp.int32)
    token_ids = jnp.arange(TOKENS, dtype=jnp.int32)
    block_index = token_ids // TOK_DEV
    source = block_index // SPLITS
    split_index = block_index % SPLITS
    per_expert = SPLITS * WAVE * CAP
    slot_total = WAVE * per_expert
    position = wave_ids[None, :] * per_expert + (split_index[:, None] * WAVE + source[:, None]) * CAP + places
    position = position.astype(jnp.int32)
    target = jnp.where(member > 0, position, slot_total).reshape(-1)
    token_table = jnp.full((slot_total,), TOKENS, jnp.int32).at[target].set(
        jnp.broadcast_to(token_ids[:, None], (TOKENS, WAVE)).reshape(-1), mode="drop")
    gate_table = jnp.zeros((slot_total,), jnp.float32).at[target].set(gate_by_expert.reshape(-1), mode="drop")
    padded = jnp.concatenate([grad_out, jnp.zeros((1, D), grad_out.dtype)], axis=0)

    def one_expert(inputs):
        weight, tokens_here, gates_here, saved_here = inputs
        arrived = padded[tokens_here].astype(jnp.float32)
        grad_hidden = lax.dot_general(arrived, weight.astype(jnp.float32), (((1,), (1,)), ((), ())),
                                      precision=lax.Precision.HIGHEST)
        flat_saved = saved_here.reshape(per_expert, 2 * FF)
        gate_pre = flat_saved[:, :FF].astype(jnp.float32)
        up_pre = flat_saved[:, FF:].astype(jnp.float32)
        sigmoid_gate = jax.nn.sigmoid(gate_pre)
        silu_gate = gate_pre * sigmoid_gate
        hidden = (silu_gate * up_pre).astype(jnp.bfloat16)
        score_values = jnp.sum(grad_hidden * lax.optimization_barrier(hidden).astype(jnp.float32), axis=1)
        scaled = grad_hidden * gates_here[:, None]
        grad_gate_pre = scaled * up_pre * sigmoid_gate * (1.0 + gate_pre * (1.0 - sigmoid_gate))
        grad_up_pre = scaled * silu_gate
        grad_pre = jnp.concatenate([grad_gate_pre, grad_up_pre], axis=1).astype(jnp.bfloat16)
        return grad_pre.reshape(SPLITS, WAVE * CAP, 2 * FF), score_values

    grad_pre, score_values = lax.map(one_expert, (w_down, token_table.reshape(WAVE, per_expert),
                                            gate_table.reshape(WAVE, per_expert), saved))
    route_position = jnp.take_along_axis(position, owners, axis=1)
    routing_weights = score_values.reshape(-1)[jnp.clip(route_position, 0, slot_total - 1)]
    grad_gate = jnp.where(flight, routing_weights, jnp.zeros_like(routing_weights))
    return grad_pre, grad_gate
```

```python
import functools

import jax
import jax.numpy as jnp
from jax import lax
from jax.experimental import pallas as pl
from jax.experimental.pallas import tpu as pltpu
from jax.sharding import Mesh, PartitionSpec as P


LANES = 128
STEP = 8
EP = ("zh", "y")
F32, BF16 = jnp.float32, jnp.bfloat16
VMEM = pl.BlockSpec(memory_space=pltpu.VMEM)
SMEM = pl.BlockSpec(memory_space=pltpu.SMEM)


def ring(size, shift):
    return [((i + shift) % size, i) for i in range(size)]


def pack_kernel(core_ref, tokens_ref, routes_ref, gate_ref, keep_ref, send_ref):
    core = core_ref[0]
    rows = tokens_ref.shape[0]
    table = jnp.concatenate(
        [routes_ref[...].astype(F32), gate_ref[...].astype(F32)], axis=0
    ).astype(BF16)
    for ref, parity in ((keep_ref, core), (send_ref, 1 - core)):
        for b in range(ref.shape[1] // LANES):
            start = pl.multiple_of((2 * b + parity) * LANES, LANES)
            ref[:rows, b * LANES : (b + 1) * LANES] = tokens_ref[:, pl.ds(start, LANES)]
        ref[rows:, :] = jnp.zeros((table.shape[0], ref.shape[1]), BF16)
        ref[rows:, :LANES] = table


def places(routes, experts):
    tokens = routes.shape[1]
    wanted = (STEP * lax.broadcasted_iota(jnp.int32, (experts, tokens), 0)).astype(F32)
    hits = [routes[k : k + 1, :] == wanted for k in range(routes.shape[0])]
    member = functools.reduce(jnp.add, [h.astype(F32) for h in hits])
    before = lax.broadcasted_iota(jnp.int32, (tokens, tokens), 0) < lax.broadcasted_iota(
        jnp.int32, (tokens, tokens), 1
    )
    place = lax.dot_general(
        member.astype(BF16),
        before.astype(F32).astype(BF16),
        (((1,), (0,)), ((), ())),
        preferred_element_type=F32,
    )
    return hits, jnp.where(member > 0.5, place, -1.0)


def one_hot(place, capacity):
    experts, tokens = place.shape
    spread = jnp.broadcast_to(place[:, None, :], (experts, capacity, tokens))
    slot = lax.broadcasted_iota(jnp.int32, (experts, capacity, tokens), 1).astype(F32)
    return (spread == slot).astype(F32).reshape(experts * capacity, tokens)


def dispatch_kernel(core_ref, keep_ref, got_ref, out_ref):
    core = core_ref[0]
    experts = out_ref.shape[0]
    capacity = out_ref.shape[1] // 2
    width = keep_ref.shape[1]
    tokens = LANES
    for ref, side in ((keep_ref, core), (got_ref, 1 - core)):
        table = ref[tokens:, :LANES].astype(F32)
        half = table.shape[0] // 2
        routes, gate = table[:half], table[half:]
        hits, place = places(routes, experts)
        gates = functools.reduce(
            jnp.add, [jnp.where(h, gate[k : k + 1, :], 0.0) for k, h in enumerate(hits)]
        )
        chosen = one_hot(place, capacity)
        spread = jnp.broadcast_to(gates[:, None, :], (experts, capacity, tokens))
        gate_out = jnp.sum(
            chosen * spread.reshape(experts * capacity, tokens), axis=1, keepdims=True
        )
        rows = jnp.dot(chosen.astype(BF16), ref[:tokens, :], preferred_element_type=F32)
        base = pl.multiple_of(side * capacity, capacity)
        out_ref[:, pl.ds(base, capacity), :width] = rows.astype(BF16).reshape(
            experts, capacity, width
        )
        out_ref[:, pl.ds(base, capacity), width:] = (
            jnp.broadcast_to(gate_out, (experts * capacity, LANES))
            .astype(BF16)
            .reshape(experts, capacity, LANES)
        )


def matmul_kernel(shifts, info_ref, arrived_ref, *refs):
    weights, (theirs_ref, mine_ref, rows_ref) = refs[:-3], refs[-3:]
    core = info_ref[0]
    sources, pair, _ = arrived_ref.shape
    capacity = pair // 2
    slots = sources * capacity
    parts = [(w, i) for w in weights for i in range(w.shape[0])]
    for half, side in ((0, 1 - core), (1, core)):
        base = pl.multiple_of(side * capacity, capacity)
        for n, (dz, dx) in enumerate(shifts):
            chip = ((info_ref[1] + dz) & 3) * 4 + ((info_ref[2] + dx) & 3)
            start = pl.multiple_of(chip * LANES, LANES)
            rows_ref[half * slots : (half + 1) * slots, n * LANES : (n + 1) * LANES] = (
                arrived_ref[:, pl.ds(base, capacity), pl.ds(start, LANES)].reshape(slots, LANES)
            )
    step = 256
    for j in range(mine_ref.shape[1] // step):
        cols = slice(j * step, (j + 1) * step)
        block = jnp.concatenate([w[i, cols, :] for w, i in parts], axis=1)
        out = lax.dot_general(
            rows_ref[...], block, (((1,), (1,)), ((), ())), preferred_element_type=F32
        )
        theirs_ref[:, cols] = out[:slots]
        mine_ref[:, cols] = out[slots:]


def finish_kernel(mine_ref, theirs_ref, saved_ref, gate_ref, out_ref, score_ref):
    rows, units = mine_ref.shape
    step = 256
    total = jnp.zeros((rows, 1), F32)
    gate_in = gate_ref[...].reshape(rows, LANES)[:, :1].astype(F32)
    for j in range(units // step):
        cols = slice(j * step, (j + 1) * step)
        up_cols = slice(units + j * step, units + (j + 1) * step)
        grad = mine_ref[:, cols] + theirs_ref[:, cols]
        a = saved_ref[:, cols].astype(F32)
        u = saved_ref[:, up_cols].astype(F32)
        sig = 1.0 / (1.0 + jnp.exp(-a))
        silu = a * sig
        hidden = (silu * u).astype(BF16).astype(F32)
        total += jnp.sum(grad * hidden, axis=1, keepdims=True)
        scaled = grad * gate_in
        out_ref[:, cols] = (scaled * u * sig * (1.0 + a * (1.0 - sig))).astype(BF16)
        out_ref[:, up_cols] = (scaled * silu).astype(BF16)
    sources, _, lanes = score_ref.shape
    capacity = rows // sources
    shape = (sources, capacity, lanes)
    spread = jnp.broadcast_to(total, (rows, lanes)).reshape(shape)
    same = lax.broadcasted_iota(jnp.int32, shape, 1) == lax.broadcasted_iota(jnp.int32, shape, 2)
    line = jnp.sum(jnp.where(same, spread, 0.0), axis=1, keepdims=True)
    score_ref[...] = jnp.broadcast_to(line, score_ref.shape)


def home_kernel(routes_ref, back_ref, out_ref):
    experts = back_ref.shape[0]
    capacity = experts * 0 + CAPACITY
    routes = routes_ref[...].astype(F32)
    hits, place = places(routes, experts)
    chosen = one_hot(place, capacity)
    shape = (experts, capacity, LANES)
    line = jnp.broadcast_to(back_ref[:, :1, :], shape)
    same = lax.broadcasted_iota(jnp.int32, shape, 1) == lax.broadcasted_iota(jnp.int32, shape, 2)
    column = jnp.sum(jnp.where(same, line, 0.0), axis=2, keepdims=True)
    score = jnp.sum(column * chosen.reshape(experts, capacity, -1), axis=1)
    for k, h in enumerate(hits):
        out_ref[k : k + 1, :] = jnp.sum(jnp.where(h, score, 0.0), axis=0, keepdims=True)


CAPACITY = 16


def call(kernel, shapes, in_specs, out_specs, scratch=()):
    return pl.pallas_call(
        kernel,
        out_shape=shapes,
        in_specs=in_specs,
        out_specs=out_specs,
        scratch_shapes=list(scratch),
    )


def gather_weights(block):
    x = lambda b, r: lax.ppermute(b, "x", ring(4, r))
    z = lambda b, r: lax.ppermute(b, "zl", ring(4, r))
    z1, z3 = z(block, 1), z(block, 3)
    z2 = z(block, 2)
    first = [block] + [x(block, r) for r in (1, 3, 2)]
    pair = jnp.concatenate([z1, z3], axis=0)
    second = [pair] + [x(pair, r) for r in (1, 3, 2)]
    third = [z2] + [x(z2, r) for r in (1, 3, 2)]
    groups, shifts = [], []
    for arrays, zs in ((first, (0,)), (second, (1, 3)), (third, (2,))):
        for array, r in zip(arrays, (0, 1, 3, 2)):
            groups.append(array)
            shifts += [(dz, r) for dz in zs]
    return groups, shifts


def on_device(grad_out, routes, gate, saved, w_down):
    tokens, width = grad_out.shape
    units, slots = w_down.shape[1], saved.shape[2]
    sources = slots // CAPACITY
    core = lax.axis_index("c")
    groups, shifts = gather_weights(w_down)
    info = jnp.stack([core, lax.axis_index("zl"), lax.axis_index("x")]).astype(jnp.int32)
    half = width // 2
    routes_t, gate_t = routes.T, gate.T
    packed = jax.ShapeDtypeStruct((tokens + 16, half), BF16)
    keep, send = call(pack_kernel, (packed, packed), [SMEM, VMEM, VMEM, VMEM], (VMEM, VMEM))(
        info, grad_out, routes_t, gate_t
    )
    got = lax.ppermute(send, "c", ring(2, 1))
    outgoing = call(
        dispatch_kernel,
        jax.ShapeDtypeStruct((sources, 2 * CAPACITY, half + LANES), BF16),
        [SMEM, VMEM, VMEM],
        VMEM,
    )(info, keep, got)
    arrived = lax.all_to_all(outgoing, EP, split_axis=0, concat_axis=0, tiled=True)
    product = jax.ShapeDtypeStruct((slots, units), F32)
    theirs, mine = call(
        functools.partial(matmul_kernel, shifts),
        (product, product),
        [SMEM] + [VMEM] * (1 + len(groups)),
        (VMEM, VMEM),
        [pltpu.VMEM((2 * slots, half), BF16)],
    )(info, arrived, *groups)
    theirs = lax.ppermute(theirs, "c", ring(2, 1))
    gate_in = lax.dynamic_slice(
        arrived, (0, core * CAPACITY, half), (sources, CAPACITY, LANES)
    )
    grad_pre, score = call(
        finish_kernel,
        (
            jax.ShapeDtypeStruct((slots, 2 * units), BF16),
            jax.ShapeDtypeStruct((sources, 8, LANES), F32),
        ),
        [VMEM] * 4,
        (VMEM, VMEM),
    )(mine, theirs, saved[0, 0], gate_in)
    back = lax.all_to_all(score, EP, split_axis=0, concat_axis=0, tiled=True)
    grad_gate = call(
        home_kernel, jax.ShapeDtypeStruct((routes.shape[1], tokens), F32), [VMEM, VMEM], VMEM
    )(routes_t, back)
    return grad_pre.reshape(saved.shape), grad_gate.T


def solution(mesh):
    fine = Mesh(mesh.devices.reshape(2, 8, 4, 4, 2), ("zh", "y", "zl", "x", "c"))
    sp = ("zl", "x", "c")
    in_specs = (
        P(EP + sp, None),
        P(EP + sp, None),
        P(EP + sp, None),
        P(EP, sp, None, None),
        P(EP, None, sp),
    )
    out_specs = (P(EP, sp, None, None), P(EP + sp, None))
    return jax.shard_map(
        on_device, mesh=fine, in_specs=in_specs, out_specs=out_specs, check_vma=False
    )
```

```python
import functools

import jax
import jax.numpy as jnp
from jax import lax
from jax.experimental import pallas as pl
from jax.experimental.pallas import tpu as pltpu
from jax.sharding import Mesh, PartitionSpec as P


LANES = 128
STEP = 8
EP = ("zh", "y")
F32, BF16 = jnp.float32, jnp.bfloat16
VMEM = pl.BlockSpec(memory_space=pltpu.VMEM)
SMEM = pl.BlockSpec(memory_space=pltpu.SMEM)


def ring(size, shift):
    return [((i + shift) % size, i) for i in range(size)]


def pack_kernel(core_ref, tokens_ref, routes_ref, gate_ref, keep_ref, send_ref):
    core = core_ref[0]
    rows = tokens_ref.shape[0]
    table = jnp.concatenate(
        [routes_ref[...].astype(F32), gate_ref[...].astype(F32)], axis=0
    ).astype(BF16)
    for ref, parity in ((keep_ref, core), (send_ref, 1 - core)):
        for b in range(ref.shape[1] // LANES):
            start = pl.multiple_of((2 * b + parity) * LANES, LANES)
            ref[:rows, b * LANES : (b + 1) * LANES] = tokens_ref[:, pl.ds(start, LANES)]
        ref[rows:, :] = jnp.zeros((table.shape[0], ref.shape[1]), BF16)
        ref[rows:, :LANES] = table


def places(routes, experts):
    tokens = routes.shape[1]
    wanted = (STEP * lax.broadcasted_iota(jnp.int32, (experts, tokens), 0)).astype(F32)
    hits = [routes[k : k + 1, :] == wanted for k in range(routes.shape[0])]
    member = functools.reduce(jnp.add, [h.astype(F32) for h in hits])
    before = lax.broadcasted_iota(jnp.int32, (tokens, tokens), 0) < lax.broadcasted_iota(
        jnp.int32, (tokens, tokens), 1
    )
    place = lax.dot_general(
        member.astype(BF16),
        before.astype(F32).astype(BF16),
        (((1,), (0,)), ((), ())),
        preferred_element_type=F32,
    )
    return hits, jnp.where(member > 0.5, place, -1.0)


def one_hot(place, capacity):
    experts, tokens = place.shape
    spread = jnp.broadcast_to(place[:, None, :], (experts, capacity, tokens))
    slot = lax.broadcasted_iota(jnp.int32, (experts, capacity, tokens), 1).astype(F32)
    return (spread == slot).astype(F32).reshape(experts * capacity, tokens)


def eye(shape):
    return lax.broadcasted_iota(jnp.int32, shape, 1) == lax.broadcasted_iota(jnp.int32, shape, 2)


def to_lanes(column, sources):
    rows = column.shape[0]
    shape = (sources, rows // sources, LANES)
    spread = jnp.broadcast_to(column, (rows, LANES)).reshape(shape)
    return jnp.sum(jnp.where(eye(shape), spread, 0.0), axis=1, keepdims=True)


def to_column(line, capacity):
    sources = line.shape[0]
    shape = (sources, capacity, LANES)
    spread = jnp.where(eye(shape), jnp.broadcast_to(line, shape), 0.0)
    return jnp.sum(spread.reshape(sources * capacity, LANES), axis=1, keepdims=True)


def dispatch_kernel(core_ref, keep_ref, got_ref, out_ref):
    core = core_ref[0]
    experts = out_ref.shape[0]
    blocks = keep_ref.shape[1] // LANES
    capacity = (out_ref.shape[1] - 8) // (2 * blocks)
    tokens = LANES
    lines = [None, None]
    for which, (ref, side) in enumerate(((keep_ref, core), (got_ref, 1 - core))):
        table = ref[tokens:, :LANES].astype(F32)
        half = table.shape[0] // 2
        routes, gate = table[:half], table[half:]
        hits, place = places(routes, experts)
        gates = functools.reduce(
            jnp.add, [jnp.where(h, gate[k : k + 1, :], 0.0) for k, h in enumerate(hits)]
        )
        chosen = one_hot(place, capacity)
        spread = jnp.broadcast_to(gates[:, None, :], (experts, capacity, tokens))
        column = jnp.sum(
            chosen * spread.reshape(experts * capacity, tokens), axis=1, keepdims=True
        )
        lines[which] = to_lanes(column, experts)
        rows = jnp.dot(chosen.astype(BF16), ref[:tokens, :], preferred_element_type=F32)
        rows = rows.astype(BF16)
        for b in range(blocks):
            base = pl.multiple_of(2 * capacity * b + side * capacity, capacity)
            out_ref[:, pl.ds(base, capacity), :] = rows[:, b * LANES : (b + 1) * LANES].reshape(
                experts, capacity, LANES
            )
    tile = (experts, 8, LANES)
    first = lax.broadcasted_iota(jnp.int32, tile, 1) == core
    out_ref[:, 2 * capacity * blocks :, :] = jnp.where(
        first, jnp.broadcast_to(lines[0], tile), jnp.broadcast_to(lines[1], tile)
    ).astype(BF16)


def matmul_kernel(shifts, other, info_ref, arrived_ref, *refs):
    weights, (out_ref, rows_ref) = refs[:-2], refs[-2:]
    parts = [(w, i) for w in weights for i in range(w.shape[0])]

    @pl.when(pl.program_id(0) == 0)
    def _():
        side = 1 - info_ref[0] if other else info_ref[0]
        slots = out_ref.shape[0]
        capacity = slots // arrived_ref.shape[0]
        for n, (dz, dx) in enumerate(shifts):
            chip = ((info_ref[1] + dz) & 3) * 4 + ((info_ref[2] + dx) & 3)
            start = pl.multiple_of(2 * capacity * chip + capacity * side, capacity)
            rows_ref[:, n * LANES : (n + 1) * LANES] = arrived_ref[
                :, pl.ds(start, capacity), :
            ].reshape(slots, LANES)

    block = jnp.concatenate([w[i] for w, i in parts], axis=1)
    out_ref[...] = lax.dot_general(
        rows_ref[...], block, (((1,), (1,)), ((), ())), preferred_element_type=F32
    )


def finish_kernel(info_ref, mine_ref, theirs_ref, saved_ref, gate_ref, out_ref, score_ref):
    rows, units = mine_ref.shape
    here = pl.ds(pl.multiple_of(pl.program_id(0) * rows, rows), rows)
    sources = score_ref.shape[0]
    step = 256
    total = jnp.zeros((rows, 1), F32)
    tile = gate_ref[...].astype(F32)
    mine = lax.broadcasted_iota(jnp.int32, tile.shape, 1) == info_ref[0]
    line = jnp.sum(jnp.where(mine, tile, 0.0), axis=1, keepdims=True)
    gate_in = to_column(line, rows // sources)
    for j in range(units // step):
        cols = slice(j * step, (j + 1) * step)
        up_cols = slice(units + j * step, units + (j + 1) * step)
        grad = mine_ref[:, cols] + theirs_ref[here, cols]
        a = saved_ref[:, cols].astype(F32)
        u = saved_ref[:, up_cols].astype(F32)
        sig = 1.0 / (1.0 + jnp.exp(-a))
        silu = a * sig
        hidden = (silu * u).astype(BF16).astype(F32)
        total += jnp.sum(grad * hidden, axis=1, keepdims=True)
        scaled = grad * gate_in
        out_ref[:, cols] = (scaled * u * sig * (1.0 + a * (1.0 - sig))).astype(BF16)
        out_ref[:, up_cols] = (scaled * silu).astype(BF16)
    score_ref[...] = jnp.broadcast_to(to_lanes(total, sources), score_ref.shape)


def home_kernel(routes_ref, back_ref, out_ref):
    experts = back_ref.shape[0]
    routes = routes_ref[...].astype(F32)
    hits, place = places(routes, experts)
    chosen = one_hot(place, CAPACITY)
    column = to_column(back_ref[:, :1, :], CAPACITY)
    score = jnp.sum((column * chosen).reshape(experts, CAPACITY, -1), axis=1)
    for k, h in enumerate(hits):
        out_ref[k : k + 1, :] = jnp.sum(jnp.where(h, score, 0.0), axis=0, keepdims=True)


CAPACITY = 16


def call(kernel, shapes, in_specs, out_specs, scratch=(), grid=()):
    return pl.pallas_call(
        kernel,
        out_shape=shapes,
        grid=grid,
        in_specs=in_specs,
        out_specs=out_specs,
        scratch_shapes=list(scratch),
        compiler_params=pltpu.CompilerParams(vmem_limit_bytes=24 << 20),
    )


def near(array):
    return pltpu.with_memory_space_constraint(array, pltpu.VMEM)


def far(array):
    return pltpu.with_memory_space_constraint(array, pltpu.HBM)


def permute(array, axis, shift):
    return lax.ppermute(array, axis, ring(4, shift))


def gather_weights(block):
    z1, z3, z2 = (permute(block, "zl", r) for r in (1, 3, 2))
    first = [block] + [permute(block, "x", r) for r in (1, 3, 2)]
    pair = jnp.concatenate([z1, z3], axis=0)
    second = [pair] + [permute(pair, "x", r) for r in (1, 3, 2)]
    third = [z2] + [permute(z2, "x", r) for r in (1, 3, 2)]
    groups, shifts = [], []
    for arrays, zs in ((first, (0,)), (second, (1, 3)), (third, (2,))):
        for array, r in zip(arrays, (0, 1, 3, 2)):
            groups.append(array)
            shifts += [(dz, r) for dz in zs]
    return groups, shifts


def step(grad_out, routes, gate, saved, w_down):
    tokens, width = grad_out.shape
    units, slots = w_down.shape[1], saved.shape[2]
    sources = slots // CAPACITY
    groups, shifts = gather_weights(w_down)
    info = jnp.stack([lax.axis_index(a) for a in ("c", "zl", "x")]).astype(jnp.int32)
    half = width // 2
    blocks = half // LANES
    routes_t, gate_t = routes.T, gate.T
    packed = jax.ShapeDtypeStruct((tokens + 16, half), BF16)
    keep, send = call(pack_kernel, (packed, packed), [SMEM, VMEM, VMEM, VMEM], (VMEM, VMEM))(
        info, grad_out, routes_t, gate_t
    )
    got = lax.ppermute(send, "c", ring(2, 1))
    outgoing = call(
        dispatch_kernel,
        jax.ShapeDtypeStruct((sources, 2 * CAPACITY * blocks + 8, LANES), BF16),
        [SMEM, VMEM, VMEM],
        VMEM,
    )(info, keep, got)
    arrived = lax.all_to_all(outgoing, EP, split_axis=0, concat_axis=0, tiled=True)
    part = 256
    theirs, mine = (
        call(
            functools.partial(matmul_kernel, shifts, other),
            jax.ShapeDtypeStruct((slots, units), F32),
            [SMEM, VMEM]
            + [pl.BlockSpec((g.shape[0], part, LANES), lambda j: (0, j, 0)) for g in groups],
            pl.BlockSpec((slots, part), lambda j: (0, j)),
            [pltpu.VMEM((slots, half), BF16)],
            (units // part,),
        )(info, near(arrived), *map(far, groups))
        for other in (True, False)
    )
    theirs = lax.ppermute(theirs, "c", ring(2, 1))
    gates = arrived[:, 2 * CAPACITY * blocks :, :]
    steps = 4
    rows = slots // steps
    tile = pl.BlockSpec((sources // steps, 8, LANES), lambda i: (i, 0, 0))
    wide = pl.BlockSpec((rows, 2 * units), lambda i: (i, 0))
    grad_pre, score = call(
        finish_kernel,
        (
            jax.ShapeDtypeStruct((slots, 2 * units), BF16),
            jax.ShapeDtypeStruct((sources, 8, LANES), F32),
        ),
        [SMEM, pl.BlockSpec((rows, units), lambda i: (i, 0)), VMEM, wide, tile],
        (wide, tile),
        grid=(steps,),
    )(info, mine, near(theirs), saved[0, 0], gates)
    back = lax.all_to_all(score, EP, split_axis=0, concat_axis=0, tiled=True)
    grad_gate = call(
        home_kernel, jax.ShapeDtypeStruct((routes.shape[1], tokens), F32), [VMEM, VMEM], VMEM
    )(routes_t, back)
    return grad_pre.reshape(saved.shape), grad_gate.T


def solution(mesh):
    fine = Mesh(mesh.devices.reshape(2, 8, 4, 4, 2), ("zh", "y", "zl", "x", "c"))
    sp = ("zl", "x", "c")
    in_specs = (
        P(EP + sp, None),
        P(EP + sp, None),
        P(EP + sp, None),
        P(EP, sp, None, None),
        P(EP, None, sp),
    )
    out_specs = (P(EP, sp, None, None), P(EP + sp, None))
    return jax.shard_map(step, mesh=fine, in_specs=in_specs, out_specs=out_specs, check_vma=False)
```

```python
import functools

import jax
import jax.numpy as jnp
from jax import lax
from jax.experimental import pallas as pl
from jax.experimental.pallas import tpu as pltpu
from jax.sharding import Mesh, PartitionSpec as P


LANES = 128
STEP = 8
EP = ("zh", "y")
F32, BF16 = jnp.float32, jnp.bfloat16
VMEM = pl.BlockSpec(memory_space=pltpu.VMEM)
SMEM = pl.BlockSpec(memory_space=pltpu.SMEM)


def ring(size, shift):
    return [((i + shift) % size, i) for i in range(size)]


def pack_kernel(core_ref, tokens_ref, routes_ref, gate_ref, keep_ref, send_ref):
    core = core_ref[0]
    rows = tokens_ref.shape[0]
    table = jnp.concatenate(
        [routes_ref[...].astype(F32), gate_ref[...].astype(F32)], axis=0
    ).astype(BF16)
    for ref, parity in ((keep_ref, core), (send_ref, 1 - core)):
        for b in range(ref.shape[1] // LANES):
            start = pl.multiple_of((2 * b + parity) * LANES, LANES)
            ref[:rows, b * LANES : (b + 1) * LANES] = tokens_ref[:, pl.ds(start, LANES)]
        ref[rows:, :] = jnp.zeros((table.shape[0], ref.shape[1]), BF16)
        ref[rows:, :LANES] = table


def places(routes, experts):
    tokens = routes.shape[1]
    wanted = (STEP * lax.broadcasted_iota(jnp.int32, (experts, tokens), 0)).astype(F32)
    hits = [routes[k : k + 1, :] == wanted for k in range(routes.shape[0])]
    member = functools.reduce(jnp.add, [h.astype(F32) for h in hits])
    before = lax.broadcasted_iota(jnp.int32, (tokens, tokens), 0) < lax.broadcasted_iota(
        jnp.int32, (tokens, tokens), 1
    )
    place = lax.dot_general(
        member.astype(BF16),
        before.astype(F32).astype(BF16),
        (((1,), (0,)), ((), ())),
        preferred_element_type=F32,
    )
    return hits, jnp.where(member > 0.5, place, -1.0)


def one_hot(place, capacity):
    experts, tokens = place.shape
    spread = jnp.broadcast_to(place[:, None, :], (experts, capacity, tokens))
    slot = lax.broadcasted_iota(jnp.int32, (experts, capacity, tokens), 1).astype(F32)
    return (spread == slot).astype(F32).reshape(experts * capacity, tokens)


def eye(shape):
    return lax.broadcasted_iota(jnp.int32, shape, 1) == lax.broadcasted_iota(jnp.int32, shape, 2)


def to_lanes(column, sources):
    rows = column.shape[0]
    shape = (sources, rows // sources, LANES)
    spread = jnp.broadcast_to(column, (rows, LANES)).reshape(shape)
    return jnp.sum(jnp.where(eye(shape), spread, 0.0), axis=1, keepdims=True)


def to_column(line, capacity):
    sources = line.shape[0]
    shape = (sources, capacity, LANES)
    spread = jnp.where(eye(shape), jnp.broadcast_to(line, shape), 0.0)
    return jnp.sum(spread.reshape(sources * capacity, LANES), axis=1, keepdims=True)


def dispatch_kernel(core_ref, keep_ref, got_ref, out_ref):
    core = core_ref[0]
    experts = out_ref.shape[0]
    blocks = keep_ref.shape[1] // LANES
    capacity = (out_ref.shape[1] - 8) // (2 * blocks)
    tokens = LANES
    lines = [None, None]
    for which, (ref, side) in enumerate(((keep_ref, core), (got_ref, 1 - core))):
        table = ref[tokens:, :LANES].astype(F32)
        half = table.shape[0] // 2
        routes, gate = table[:half], table[half:]
        hits, place = places(routes, experts)
        gates = functools.reduce(
            jnp.add, [jnp.where(h, gate[k : k + 1, :], 0.0) for k, h in enumerate(hits)]
        )
        chosen = one_hot(place, capacity)
        spread = jnp.broadcast_to(gates[:, None, :], (experts, capacity, tokens))
        column = jnp.sum(
            chosen * spread.reshape(experts * capacity, tokens), axis=1, keepdims=True
        )
        lines[which] = to_lanes(column, experts)
        rows = jnp.dot(chosen.astype(BF16), ref[:tokens, :], preferred_element_type=F32)
        rows = rows.astype(BF16)
        for b in range(blocks):
            base = pl.multiple_of(2 * capacity * b + side * capacity, capacity)
            out_ref[:, pl.ds(base, capacity), :] = rows[:, b * LANES : (b + 1) * LANES].reshape(
                experts, capacity, LANES
            )
    tile = (experts, 8, LANES)
    first = lax.broadcasted_iota(jnp.int32, tile, 1) == core
    out_ref[:, 2 * capacity * blocks :, :] = jnp.where(
        first, jnp.broadcast_to(lines[0], tile), jnp.broadcast_to(lines[1], tile)
    ).astype(BF16)


def matmul_kernel(shifts, other, more, info_ref, arrived_ref, *refs):
    refs, (out_ref, rows_ref) = refs[:-2], refs[-2:]
    weights = refs[1:] if more else refs
    parts = [(w, i) for w in weights for i in range(w.shape[0])]

    @pl.when(pl.program_id(0) == 0)
    def _():
        side = 1 - info_ref[0] if other else info_ref[0]
        slots = out_ref.shape[0]
        capacity = slots // arrived_ref.shape[0]
        for n, (dz, dx) in enumerate(shifts):
            chip = ((info_ref[1] + dz) & 3) * 4 + ((info_ref[2] + dx) & 3)
            start = pl.multiple_of(2 * capacity * chip + capacity * side, capacity)
            rows_ref[:, n * LANES : (n + 1) * LANES] = arrived_ref[
                :, pl.ds(start, capacity), :
            ].reshape(slots, LANES)

    block = jnp.concatenate([w[i] for w, i in parts], axis=1)
    out = lax.dot_general(
        rows_ref[...], block, (((1,), (1,)), ((), ())), preferred_element_type=F32
    )
    out_ref[...] = refs[0][...] + out if more else out


def finish_kernel(info_ref, mine_ref, theirs_ref, saved_ref, gate_ref, out_ref, score_ref):
    rows, units = mine_ref.shape
    here = pl.ds(pl.multiple_of(pl.program_id(0) * rows, rows), rows)
    sources = score_ref.shape[0]
    step = 256
    total = jnp.zeros((rows, 1), F32)
    tile = gate_ref[...].astype(F32)
    mine = lax.broadcasted_iota(jnp.int32, tile.shape, 1) == info_ref[0]
    line = jnp.sum(jnp.where(mine, tile, 0.0), axis=1, keepdims=True)
    gate_in = to_column(line, rows // sources)
    for j in range(units // step):
        cols = slice(j * step, (j + 1) * step)
        up_cols = slice(units + j * step, units + (j + 1) * step)
        grad = mine_ref[:, cols] + theirs_ref[here, cols]
        a = saved_ref[:, cols].astype(F32)
        u = saved_ref[:, up_cols].astype(F32)
        sig = 1.0 / (1.0 + jnp.exp(-a))
        silu = a * sig
        hidden = (silu * u).astype(BF16).astype(F32)
        total += jnp.sum(grad * hidden, axis=1, keepdims=True)
        scaled = grad * gate_in
        out_ref[:, cols] = (scaled * u * sig * (1.0 + a * (1.0 - sig))).astype(BF16)
        out_ref[:, up_cols] = (scaled * silu).astype(BF16)
    score_ref[...] = jnp.broadcast_to(to_lanes(total, sources), score_ref.shape)


def home_kernel(routes_ref, back_ref, out_ref):
    experts = back_ref.shape[0]
    routes = routes_ref[...].astype(F32)
    hits, place = places(routes, experts)
    chosen = one_hot(place, CAPACITY)
    column = to_column(back_ref[:, :1, :], CAPACITY)
    score = jnp.sum((column * chosen).reshape(experts, CAPACITY, -1), axis=1)
    for k, h in enumerate(hits):
        out_ref[k : k + 1, :] = jnp.sum(jnp.where(h, score, 0.0), axis=0, keepdims=True)


CAPACITY = 16


def call(kernel, shapes, in_specs, out_specs, scratch=(), grid=()):
    return pl.pallas_call(
        kernel,
        out_shape=shapes,
        grid=grid,
        in_specs=in_specs,
        out_specs=out_specs,
        scratch_shapes=list(scratch),
        compiler_params=pltpu.CompilerParams(vmem_limit_bytes=24 << 20),
    )


def near(array):
    return pltpu.with_memory_space_constraint(array, pltpu.VMEM)


def far(array):
    return pltpu.with_memory_space_constraint(array, pltpu.HBM)


def permute(array, axis, shift):
    return lax.ppermute(array, axis, ring(4, shift))


def gather_weights(block):
    z1, z3, z2 = (permute(block, "zl", r) for r in (1, 3, 2))
    trio = jnp.concatenate([block, z1, z3], axis=0)
    up, down = permute(trio, "x", 1), permute(trio, "x", 3)
    up2, down2 = permute(z2, "x", 1), permute(z2, "x", 3)
    far1 = permute(up[:2], "x", 1)
    far3 = permute(down[2:], "x", 3)
    last = permute(down2, "x", 3)
    early = [(trio, (0, 1, 3), 0), (z2, (2,), 0), (up, (0, 1, 3), 1)]
    early += [(down, (0, 1, 3), 3), (up2, (2,), 1), (down2, (2,), 3)]
    late = [(far1, (0, 1), 2), (far3, (3,), 2), (last, (2,), 2)]
    return early, late


def step(grad_out, routes, gate, saved, w_down):
    tokens, width = grad_out.shape
    units, slots = w_down.shape[1], saved.shape[2]
    sources = slots // CAPACITY
    early, late = gather_weights(w_down)
    info = jnp.stack([lax.axis_index(a) for a in ("c", "zl", "x")]).astype(jnp.int32)
    half = width // 2
    blocks = half // LANES
    routes_t, gate_t = routes.T, gate.T
    packed = jax.ShapeDtypeStruct((tokens + 16, half), BF16)
    keep, send = call(pack_kernel, (packed, packed), [SMEM, VMEM, VMEM, VMEM], (VMEM, VMEM))(
        info, far(grad_out), far(routes_t), far(gate_t)
    )
    got = lax.ppermute(send, "c", ring(2, 1))
    outgoing = call(
        dispatch_kernel,
        jax.ShapeDtypeStruct((sources, 2 * CAPACITY * blocks + 8, LANES), BF16),
        [SMEM, VMEM, VMEM],
        VMEM,
    )(info, keep, got)
    arrived = lax.all_to_all(outgoing, EP, split_axis=0, concat_axis=0, tiled=True)
    part = 256
    piece = pl.BlockSpec((slots, part), lambda j: (0, j))

    def product(groups, other, *more):
        shifts = [(dz, dx) for _, dzs, dx in groups for dz in dzs]
        arrays = [a for a, _, _ in groups]
        return call(
            functools.partial(matmul_kernel, shifts, other, bool(more)),
            jax.ShapeDtypeStruct((slots, units), F32),
            [SMEM, VMEM]
            + [piece] * len(more)
            + [pl.BlockSpec((a.shape[0], part, LANES), lambda j: (0, j, 0)) for a in arrays],
            piece,
            [pltpu.VMEM((slots, len(shifts) * LANES), BF16)],
            (units // part,),
        )(info, near(arrived), *more, *map(far, arrays))

    theirs = product(late, True, product(early, True))
    mine = product(early + late, False)
    theirs = lax.ppermute(theirs, "c", ring(2, 1))
    gates = arrived[:, 2 * CAPACITY * blocks :, :]
    steps = 4
    rows = slots // steps
    tile = pl.BlockSpec((sources // steps, 8, LANES), lambda i: (i, 0, 0))
    wide = pl.BlockSpec((rows, 2 * units), lambda i: (i, 0))
    grad_pre, score = call(
        finish_kernel,
        (
            jax.ShapeDtypeStruct((slots, 2 * units), BF16),
            jax.ShapeDtypeStruct((sources, 8, LANES), F32),
        ),
        [SMEM, pl.BlockSpec((rows, units), lambda i: (i, 0)), VMEM, wide, tile],
        (wide, tile),
        grid=(steps,),
    )(info, mine, near(theirs), saved[0, 0], gates)
    back = lax.all_to_all(score, EP, split_axis=0, concat_axis=0, tiled=True)
    grad_gate = call(
        home_kernel, jax.ShapeDtypeStruct((routes.shape[1], tokens), F32), [VMEM, VMEM], VMEM
    )(routes_t, back)
    return grad_pre.reshape(saved.shape), grad_gate.T


def solution(mesh):
    fine = Mesh(mesh.devices.reshape(2, 8, 4, 4, 2), ("zh", "y", "zl", "x", "c"))
    sp = ("zl", "x", "c")
    in_specs = (
        P(EP + sp, None),
        P(EP + sp, None),
        P(EP + sp, None),
        P(EP, sp, None, None),
        P(EP, None, sp),
    )
    out_specs = (P(EP, sp, None, None), P(EP + sp, None))
    return jax.shard_map(step, mesh=fine, in_specs=in_specs, out_specs=out_specs, check_vma=False)
```

```python
import functools

import jax
import jax.numpy as jnp
from jax import lax
from jax.experimental import pallas as pl
from jax.experimental.pallas import tpu as pltpu
from jax.sharding import Mesh, PartitionSpec as P


LANES = 128
CAPACITY = 16
STEP = 8
EP = ("zh", "y")
F32, BF16 = jnp.float32, jnp.bfloat16
VMEM = pl.BlockSpec(memory_space=pltpu.VMEM)
SMEM = pl.BlockSpec(memory_space=pltpu.SMEM)


def ring(size, shift):
    return [((i + shift) % size, i) for i in range(size)]


def pack_kernel(core_ref, tokens_ref, routes_ref, keep_ref, send_ref):
    core = core_ref[0]
    rows = tokens_ref.shape[0]
    for ref, parity in ((keep_ref, core), (send_ref, 1 - core)):
        for b in range(ref.shape[1] // LANES):
            start = pl.multiple_of((2 * b + parity) * LANES, LANES)
            ref[:rows, b * LANES : (b + 1) * LANES] = tokens_ref[:, pl.ds(start, LANES)]
    send_ref[rows:, :] = jnp.zeros((send_ref.shape[0] - rows, send_ref.shape[1]), BF16)
    routes = routes_ref[...].astype(F32)
    send_ref[rows:, :LANES] = jnp.concatenate([routes, routes], axis=0).astype(BF16)


def places(routes, experts):
    tokens = routes.shape[1]
    wanted = (STEP * lax.broadcasted_iota(jnp.int32, (experts, tokens), 0)).astype(F32)
    hits = [routes[k : k + 1, :] == wanted for k in range(routes.shape[0])]
    member = functools.reduce(jnp.add, [h.astype(F32) for h in hits])
    before = lax.broadcasted_iota(jnp.int32, (tokens, tokens), 0) < lax.broadcasted_iota(
        jnp.int32, (tokens, tokens), 1
    )
    place = lax.dot_general(
        member.astype(BF16),
        before.astype(F32).astype(BF16),
        (((1,), (0,)), ((), ())),
        preferred_element_type=F32,
    )
    return hits, jnp.where(member > 0.5, place, -1.0)


def one_hot(place, capacity):
    experts, tokens = place.shape
    spread = jnp.broadcast_to(place[:, None, :], (experts, capacity, tokens))
    slot = lax.broadcasted_iota(jnp.int32, (experts, capacity, tokens), 1).astype(F32)
    return (spread == slot).astype(F32).reshape(experts * capacity, tokens)


def eye(shape):
    return lax.broadcasted_iota(jnp.int32, shape, 1) == lax.broadcasted_iota(jnp.int32, shape, 2)


def to_lanes(column, sources):
    rows = column.shape[0]
    shape = (sources, rows // sources, LANES)
    spread = jnp.broadcast_to(column, (rows, LANES)).reshape(shape)
    return jnp.sum(jnp.where(eye(shape), spread, 0.0), axis=1, keepdims=True)


def to_column(line, capacity):
    sources = line.shape[0]
    shape = (sources, capacity, LANES)
    spread = jnp.where(eye(shape), jnp.broadcast_to(line, shape), 0.0)
    return jnp.sum(spread.reshape(sources * capacity, LANES), axis=1, keepdims=True)


def send_rows(place, tokens_ref, out_ref, base):
    tokens = place.shape[1]
    experts, _, lanes = out_ref.shape
    chosen = one_hot(place, CAPACITY)
    rows = jnp.dot(chosen.astype(BF16), tokens_ref[:tokens, :], preferred_element_type=F32)
    rows = rows.astype(BF16)
    for b in range(rows.shape[1] // lanes):
        start = base + b * CAPACITY
        out_ref[:, start : start + CAPACITY, :] = rows[:, b * lanes : (b + 1) * lanes].reshape(
            experts, CAPACITY, lanes
        )
    return chosen


def dispatch_kernel(got_ref, keep_ref, routes_ref, gate_ref, out_ref):
    experts = out_ref.shape[0]
    height = (out_ref.shape[1] - 8) // 2
    table = got_ref[LANES:, :LANES].astype(F32)
    _, place = places(table[: table.shape[0] // 2], experts)
    send_rows(place, got_ref, out_ref, 0)
    gate = gate_ref[...].astype(F32)
    hits, place = places(routes_ref[...].astype(F32), experts)
    chosen = send_rows(place, keep_ref, out_ref, height)
    gates = functools.reduce(
        jnp.add, [jnp.where(h, gate[k : k + 1, :], 0.0) for k, h in enumerate(hits)]
    )
    spread = jnp.broadcast_to(gates[:, None, :], (experts, CAPACITY, gates.shape[1]))
    column = jnp.sum(chosen * spread.reshape(chosen.shape), axis=1, keepdims=True)
    line = to_lanes(column, experts)
    out_ref[:, 2 * height :, :] = jnp.broadcast_to(line, (experts, 8, LANES)).astype(BF16)


def matmul_kernel(shifts, base, info_ref, arrived_ref, *refs):
    weights, (out_ref, rows_ref) = refs[:-2], refs[-2:]
    parts = [(w, i) for w in weights for i in range(w.shape[0])]

    @pl.when(pl.program_id(0) == 0)
    def _():
        slots = out_ref.shape[0]
        capacity = slots // arrived_ref.shape[0]
        for n, (dz, dx) in enumerate(shifts):
            chip = ((info_ref[1] + dz) & 3) * 4 + ((info_ref[2] + dx) & 3)
            start = pl.multiple_of(base + chip * capacity, capacity)
            rows_ref[:, n * LANES : (n + 1) * LANES] = arrived_ref[
                :, pl.ds(start, capacity), :
            ].reshape(slots, LANES)

    block = jnp.concatenate([w[i] for w, i in parts], axis=1)
    out_ref[...] = lax.dot_general(
        rows_ref[...], block, (((1,), (1,)), ((), ())), preferred_element_type=F32
    )


def finish_kernel(mine_ref, theirs_ref, saved_ref, gate_ref, out_ref, score_ref):
    rows, units = mine_ref.shape
    here = pl.ds(pl.multiple_of(pl.program_id(0) * rows, rows), rows)
    sources = score_ref.shape[0]
    step = 256
    total = jnp.zeros((rows, 1), F32)
    gate_in = to_column(gate_ref[...].astype(F32)[:, :1, :], rows // sources)
    for j in range(units // step):
        cols = slice(j * step, (j + 1) * step)
        up_cols = slice(units + j * step, units + (j + 1) * step)
        grad = mine_ref[:, cols] + theirs_ref[here, cols]
        a = saved_ref[:, cols].astype(F32)
        u = saved_ref[:, up_cols].astype(F32)
        sig = 1.0 / (1.0 + jnp.exp(-a))
        silu = a * sig
        hidden = (silu * u).astype(BF16).astype(F32)
        total += jnp.sum(grad * hidden, axis=1, keepdims=True)
        scaled = grad * gate_in
        out_ref[:, cols] = (scaled * u * sig * (1.0 + a * (1.0 - sig))).astype(BF16)
        out_ref[:, up_cols] = (scaled * silu).astype(BF16)
    score_ref[...] = jnp.broadcast_to(to_lanes(total, sources), score_ref.shape)


def home_kernel(routes_ref, back_ref, out_ref):
    experts = back_ref.shape[0]
    routes = routes_ref[...].astype(F32)
    hits, place = places(routes, experts)
    chosen = one_hot(place, CAPACITY)
    column = to_column(back_ref[:, :1, :], CAPACITY)
    score = jnp.sum((column * chosen).reshape(experts, CAPACITY, -1), axis=1)
    for k, h in enumerate(hits):
        out_ref[k : k + 1, :] = jnp.sum(jnp.where(h, score, 0.0), axis=0, keepdims=True)


def call(kernel, shapes, in_specs, out_specs, scratch=(), grid=()):
    return pl.pallas_call(
        kernel,
        out_shape=shapes,
        grid=grid,
        in_specs=in_specs,
        out_specs=out_specs,
        scratch_shapes=list(scratch),
        compiler_params=pltpu.CompilerParams(vmem_limit_bytes=24 << 20),
    )


def near(array):
    return pltpu.with_memory_space_constraint(array, pltpu.VMEM)


def far(array):
    return pltpu.with_memory_space_constraint(array, pltpu.HBM)


def permute(array, axis, shift):
    return lax.ppermute(array, axis, ring(4, shift))


def gather_weights(block):
    z1, z3, z2 = (permute(block, "zl", r) for r in (1, 3, 2))
    a1, a3 = permute(block, "x", 1), permute(block, "x", 3)
    pair = jnp.concatenate([z1, z3], axis=0)
    g1, g3 = permute(pair, "x", 1), permute(pair, "x", 3)
    a2 = permute(a1, "x", 1)
    h1, h3 = permute(z2, "x", 1), permute(z2, "x", 3)
    f1 = permute(g1[:1], "x", 1)
    f3 = permute(g3[1:], "x", 3)
    f2 = permute(h3, "x", 3)
    groups = [(block, (0,), 0), (a1, (0,), 1), (a3, (0,), 3), (a2, (0,), 2)]
    groups += [(pair, (1, 3), 0), (g1, (1, 3), 1), (g3, (1, 3), 3)]
    groups += [(z2, (2,), 0), (h1, (2,), 1), (h3, (2,), 3)]
    return groups + [(f1, (1,), 2), (f3, (3,), 2), (f2, (2,), 2)]


def step(grad_out, routes, gate, saved, w_down):
    tokens, width = grad_out.shape
    units, slots = w_down.shape[1], saved.shape[2]
    sources = slots // CAPACITY
    groups = gather_weights(w_down)
    info = jnp.stack([lax.axis_index(a) for a in ("c", "zl", "x")]).astype(jnp.int32)
    half = width // 2
    blocks = half // LANES
    routes_t, gate_t = routes.T, gate.T
    keep, send = call(
        pack_kernel,
        (
            jax.ShapeDtypeStruct((tokens, half), BF16),
            jax.ShapeDtypeStruct((tokens + 16, half), BF16),
        ),
        [SMEM, VMEM, VMEM],
        (VMEM, VMEM),
    )(info, far(grad_out), far(routes_t))
    got = lax.ppermute(send, "c", ring(2, 1))
    height = CAPACITY * blocks
    outgoing = call(
        dispatch_kernel,
        jax.ShapeDtypeStruct((sources, 2 * height + 8, LANES), BF16),
        [VMEM] * 4,
        VMEM,
    )(got, keep, far(routes_t), far(gate_t))
    arrived = lax.all_to_all(outgoing, EP, split_axis=0, concat_axis=0, tiled=True)
    part = 512
    piece = pl.BlockSpec((slots, part), lambda j: (0, j))
    shifts = [(dz, dx) for _, dzs, dx in groups for dz in dzs]
    arrays = [a for a, _, _ in groups]

    def product(base):
        return call(
            functools.partial(matmul_kernel, shifts, base),
            jax.ShapeDtypeStruct((slots, units), F32),
            [SMEM, VMEM]
            + [pl.BlockSpec((a.shape[0], part, LANES), lambda j: (0, j, 0)) for a in arrays],
            piece,
            [pltpu.VMEM((slots, half), BF16)],
            (units // part,),
        )(info, near(arrived), *map(far, arrays))

    theirs = product(0)
    mine = product(height)
    theirs = lax.ppermute(theirs, "c", ring(2, 1))
    gates = arrived[:, 2 * height :, :]
    steps = 4
    rows = slots // steps
    tile = pl.BlockSpec((sources // steps, 8, LANES), lambda i: (i, 0, 0))
    wide = pl.BlockSpec((rows, 2 * units), lambda i: (i, 0))
    grad_pre, score = call(
        finish_kernel,
        (
            jax.ShapeDtypeStruct((slots, 2 * units), BF16),
            jax.ShapeDtypeStruct((sources, 8, LANES), F32),
        ),
        [pl.BlockSpec((rows, units), lambda i: (i, 0)), VMEM, wide, tile],
        (wide, tile),
        grid=(steps,),
    )(mine, near(theirs), saved[0, 0], gates)
    back = lax.all_to_all(score, EP, split_axis=0, concat_axis=0, tiled=True)
    grad_gate = call(
        home_kernel, jax.ShapeDtypeStruct((routes.shape[1], tokens), F32), [VMEM, VMEM], VMEM
    )(routes_t, back)
    return grad_pre.reshape(saved.shape), grad_gate.T


def solution(mesh):
    fine = Mesh(mesh.devices.reshape(2, 8, 4, 4, 2), ("zh", "y", "zl", "x", "c"))
    sp = ("zl", "x", "c")
    in_specs = (
        P(EP + sp, None),
        P(EP + sp, None),
        P(EP + sp, None),
        P(EP, sp, None, None),
        P(EP, None, sp),
    )
    out_specs = (P(EP, sp, None, None), P(EP + sp, None))
    return jax.shard_map(step, mesh=fine, in_specs=in_specs, out_specs=out_specs, check_vma=False)
```

```python
import functools

import jax
import jax.numpy as jnp
from jax import lax
from jax.experimental import pallas as pl
from jax.experimental.pallas import tpu as pltpu
from jax.sharding import Mesh, PartitionSpec as P


LANES = 128
CAPACITY = 16
STEP = 8
EP = ("zh", "y")
STAY, CROSS = 3, 4
F32, BF16 = jnp.float32, jnp.bfloat16
VMEM = pl.BlockSpec(memory_space=pltpu.VMEM)
SMEM = pl.BlockSpec(memory_space=pltpu.SMEM)


def ring(size, shift):
    return [((i + shift) % size, i) for i in range(size)]


def pack_kernel(core_ref, tokens_ref, routes_ref, keep_ref, send_ref):
    core = core_ref[0]
    rows = tokens_ref.shape[0]
    for ref, parity in ((keep_ref, core), (send_ref, 1 - core)):
        for b in range(ref.shape[1] // LANES):
            start = pl.multiple_of((2 * b + parity) * LANES, LANES)
            ref[:rows, b * LANES : (b + 1) * LANES] = tokens_ref[:, pl.ds(start, LANES)]
    send_ref[rows:, :] = jnp.zeros((send_ref.shape[0] - rows, send_ref.shape[1]), BF16)
    routes = routes_ref[...].astype(F32)
    send_ref[rows:, :LANES] = jnp.concatenate([routes, routes], axis=0).astype(BF16)


def places(routes, experts, first=0):
    tokens = routes.shape[1]
    wanted = (STEP * (lax.broadcasted_iota(jnp.int32, (experts, tokens), 0) + first)).astype(F32)
    hits = [routes[k : k + 1, :] == wanted for k in range(routes.shape[0])]
    member = functools.reduce(jnp.add, [h.astype(F32) for h in hits])
    before = lax.broadcasted_iota(jnp.int32, (tokens, tokens), 0) < lax.broadcasted_iota(
        jnp.int32, (tokens, tokens), 1
    )
    place = lax.dot_general(
        member.astype(BF16),
        before.astype(F32).astype(BF16),
        (((1,), (0,)), ((), ())),
        preferred_element_type=F32,
    )
    return hits, jnp.where(member > 0.5, place, -1.0)


def one_hot(place, capacity):
    experts, tokens = place.shape
    spread = jnp.broadcast_to(place[:, None, :], (experts, capacity, tokens))
    slot = lax.broadcasted_iota(jnp.int32, (experts, capacity, tokens), 1).astype(F32)
    return (spread == slot).astype(F32).reshape(experts * capacity, tokens)


def eye(shape):
    return lax.broadcasted_iota(jnp.int32, shape, 1) == lax.broadcasted_iota(jnp.int32, shape, 2)


def to_lanes(column, sources):
    rows = column.shape[0]
    shape = (sources, rows // sources, LANES)
    spread = jnp.broadcast_to(column, (rows, LANES)).reshape(shape)
    return jnp.sum(jnp.where(eye(shape), spread, 0.0), axis=1, keepdims=True)


def to_column(line, capacity):
    sources = line.shape[0]
    shape = (sources, capacity, LANES)
    spread = jnp.where(eye(shape), jnp.broadcast_to(line, shape), 0.0)
    return jnp.sum(spread.reshape(sources * capacity, LANES), axis=1, keepdims=True)


def send_rows(place, tokens_ref, out_ref, base):
    tokens = place.shape[1]
    experts, _, lanes = out_ref.shape
    chosen = one_hot(place, CAPACITY)
    rows = jnp.dot(chosen.astype(BF16), tokens_ref[:tokens, :], preferred_element_type=F32)
    rows = rows.astype(BF16)
    for b in range(rows.shape[1] // lanes):
        start = base + b * CAPACITY
        out_ref[:, start : start + CAPACITY, :] = rows[:, b * lanes : (b + 1) * lanes].reshape(
            experts, CAPACITY, lanes
        )
    return chosen


def dispatch_kernel(side, info_ref, got_ref, keep_ref, routes_ref, gate_ref, out_ref):
    experts = out_ref.shape[0]
    first = info_ref[side] * experts
    height = (out_ref.shape[1] - 8) // 2
    table = got_ref[LANES:, :LANES].astype(F32)
    _, place = places(table[: table.shape[0] // 2], experts, first)
    send_rows(place, got_ref, out_ref, 0)
    gate = gate_ref[...].astype(F32)
    hits, place = places(routes_ref[...].astype(F32), experts, first)
    chosen = send_rows(place, keep_ref, out_ref, height)
    gates = functools.reduce(
        jnp.add, [jnp.where(h, gate[k : k + 1, :], 0.0) for k, h in enumerate(hits)]
    )
    spread = jnp.broadcast_to(gates[:, None, :], (experts, CAPACITY, gates.shape[1]))
    column = jnp.sum(chosen * spread.reshape(chosen.shape), axis=1, keepdims=True)
    line = to_lanes(column, experts)
    out_ref[:, 2 * height :, :] = jnp.broadcast_to(line, (experts, 8, LANES)).astype(BF16)


def matmul_kernel(shifts, bases, info_ref, arrived_ref, *refs):
    weights, outs, rows_ref = refs[: -1 - len(bases)], refs[-1 - len(bases) : -1], refs[-1]
    parts = [(w, i) for w in weights for i in range(w.shape[0])]
    slots = outs[0].shape[0]

    @pl.when(pl.program_id(0) == 0)
    def _():
        capacity = slots // arrived_ref.shape[0]
        for n, (dz, dx) in enumerate(shifts):
            chip = ((info_ref[1] + dz) & 3) * 4 + ((info_ref[2] + dx) & 3)
            for m, base in enumerate(bases):
                start = pl.multiple_of(base + chip * capacity, capacity)
                rows_ref[m * slots : (m + 1) * slots, n * LANES : (n + 1) * LANES] = arrived_ref[
                    :, pl.ds(start, capacity), :
                ].reshape(slots, LANES)

    block = jnp.concatenate([w[i] for w, i in parts], axis=1)
    out = lax.dot_general(
        rows_ref[...], block, (((1,), (1,)), ((), ())), preferred_element_type=F32
    )
    for m, ref in enumerate(outs):
        ref[...] = out[m * slots : (m + 1) * slots]


def finish_kernel(info_ref, mine_ref, theirs_ref, saved_ref, gate_ref, *refs):
    out_ref, score_ref = refs[-2:]
    rows, units = mine_ref.shape
    here = pl.ds(pl.multiple_of(pl.program_id(0) * rows, rows), rows)
    sources = score_ref.shape[0]
    step = 256
    total = jnp.zeros((rows, 1), F32)
    gate_in = to_column(gate_ref[...].astype(F32)[:, :1, :], rows // sources)
    for j in range(units // step):
        cols = slice(j * step, (j + 1) * step)
        up_cols = slice(units + j * step, units + (j + 1) * step)
        grad = mine_ref[:, cols] + theirs_ref[here, cols]
        a = saved_ref[:, cols].astype(F32)
        u = saved_ref[:, up_cols].astype(F32)
        sig = 1.0 / (1.0 + jnp.exp(-a))
        silu = a * sig
        hidden = (silu * u).astype(BF16).astype(F32)
        total += jnp.sum(grad * hidden, axis=1, keepdims=True)
        scaled = grad * gate_in
        out_ref[:, cols] = (scaled * u * sig * (1.0 + a * (1.0 - sig))).astype(BF16)
        out_ref[:, up_cols] = (scaled * silu).astype(BF16)
    score_ref[...] = jnp.broadcast_to(to_lanes(total, sources), score_ref.shape)


def home_kernel(routes_ref, back_ref, out_ref):
    experts = back_ref.shape[0]
    routes = routes_ref[...].astype(F32)
    hits, place = places(routes, experts)
    chosen = one_hot(place, CAPACITY)
    column = to_column(back_ref[:, :1, :], CAPACITY)
    score = jnp.sum((column * chosen).reshape(experts, CAPACITY, -1), axis=1)
    for k, h in enumerate(hits):
        out_ref[k : k + 1, :] = jnp.sum(jnp.where(h, score, 0.0), axis=0, keepdims=True)


def call(kernel, shapes, in_specs, out_specs, scratch=(), grid=(), prefetch=0, aliases=None):
    return pl.pallas_call(
        kernel,
        out_shape=shapes,
        grid_spec=pltpu.PrefetchScalarGridSpec(
            num_scalar_prefetch=prefetch,
            grid=grid,
            in_specs=in_specs,
            out_specs=out_specs,
            scratch_shapes=list(scratch),
        ),
        input_output_aliases=aliases or {},
        compiler_params=pltpu.CompilerParams(vmem_limit_bytes=24 << 20),
    )


def near(array):
    return pltpu.with_memory_space_constraint(array, pltpu.VMEM)


def far(array):
    return pltpu.with_memory_space_constraint(array, pltpu.HBM)


def permute(array, axis, shift):
    return lax.ppermute(array, axis, ring(4, shift))


def gather_weights(block):
    z1, z3, z2 = (permute(block, "zl", r) for r in (1, 3, 2))
    a1, a3 = permute(block, "x", 1), permute(block, "x", 3)
    pair = jnp.concatenate([z1, z3], axis=0)
    g1, g3 = permute(pair, "x", 1), permute(pair, "x", 3)
    a2 = permute(a1, "x", 1)
    h1, h3 = permute(z2, "x", 1), permute(z2, "x", 3)
    f1 = permute(g1[:1], "x", 1)
    f3 = permute(g3[1:], "x", 3)
    f2 = permute(h3, "x", 3)
    groups = [(block, (0,), 0), (a1, (0,), 1), (a3, (0,), 3), (a2, (0,), 2)]
    groups += [(pair, (1, 3), 0), (g1, (1, 3), 1), (g3, (1, 3), 3)]
    groups += [(z2, (2,), 0), (h1, (2,), 1), (h3, (2,), 3)]
    return groups + [(f1, (1,), 2), (f3, (3,), 2), (f2, (2,), 2)]


def step(grad_out, routes, gate, saved, w_down):
    tokens, width = grad_out.shape
    units, slots = w_down.shape[1], saved.shape[2]
    sources = slots // CAPACITY
    groups = gather_weights(w_down)
    info = jnp.stack(
        [lax.axis_index(a) for a in ("c", "zl", "x", "zh")] + [1 - lax.axis_index("zh")]
    ).astype(jnp.int32)
    half = width // 2
    blocks = half // LANES
    routes_t, gate_t = routes.T, gate.T
    keep, send = call(
        pack_kernel,
        (
            jax.ShapeDtypeStruct((tokens, half), BF16),
            jax.ShapeDtypeStruct((tokens + 16, half), BF16),
        ),
        [SMEM, VMEM, VMEM],
        (VMEM, VMEM),
    )(info, far(grad_out), far(routes_t))
    got = lax.ppermute(send, "c", ring(2, 1))
    height = CAPACITY * blocks
    peers = sources // 2

    def outgoing(side):
        return call(
            functools.partial(dispatch_kernel, side),
            jax.ShapeDtypeStruct((peers, 2 * height + 8, LANES), BF16),
            [SMEM] + [VMEM] * 4,
            VMEM,
        )(info, got, keep, far(routes_t), far(gate_t))

    def along_y(array):
        return lax.all_to_all(array, "y", split_axis=0, concat_axis=0, tiled=True)

    cross = along_y(outgoing(CROSS))
    cross = lax.ppermute(cross, "zh", ring(2, 1))
    stay = along_y(outgoing(STAY))
    part = 512
    slots = slots // 2
    piece = pl.BlockSpec((slots, part), lambda j: (0, j))
    shifts = [(dz, dx) for _, dzs, dx in groups for dz in dzs]
    arrays = [a for a, _, _ in groups]

    def products(arrived, *bases):
        return call(
            functools.partial(matmul_kernel, shifts, bases),
            (jax.ShapeDtypeStruct((slots, units), F32),) * len(bases),
            [SMEM, VMEM]
            + [pl.BlockSpec((a.shape[0], part, LANES), lambda j: (0, j, 0)) for a in arrays],
            (piece,) * len(bases),
            [pltpu.VMEM((len(bases) * slots, half), BF16)],
            (units // part,),
        )(info, near(arrived), *map(far, arrays))

    steps = 2
    rows = slots // steps

    def finish(side, arrived, mine, theirs, *before):
        tile = (peers // steps, 8, LANES)
        wide = pl.BlockSpec((rows, 2 * units), lambda i, info: (steps * info[side] + i, 0))
        score = pl.BlockSpec(tile, lambda i, info: (steps * info[side] + i, 0, 0))
        return call(
            finish_kernel,
            (
                jax.ShapeDtypeStruct((2 * slots, 2 * units), BF16),
                jax.ShapeDtypeStruct((sources, 8, LANES), F32),
            ),
            [
                pl.BlockSpec((rows, units), lambda i, info: (i, 0)),
                VMEM,
                wide,
                pl.BlockSpec(tile, lambda i, info: (i, 0, 0)),
            ]
            + [pl.BlockSpec(memory_space=pl.ANY)] * len(before),
            (wide, score),
            grid=(steps,),
            prefetch=1,
            aliases={5 + n: n for n in range(len(before))},
        )(info, mine, near(theirs), saved[0, 0], arrived[:, 2 * height :, :], *before)

    def swap(array):
        return lax.ppermute(array, "c", ring(2, 1))

    theirs, mine = products(stay, 0, height)
    theirs = swap(theirs)
    before = finish(STAY, stay, mine, theirs)
    (theirs,) = products(cross, 0)
    theirs = swap(theirs)
    (mine,) = products(cross, height)
    grad_pre, score = finish(CROSS, cross, mine, theirs, *before)
    back = lax.all_to_all(score, EP, split_axis=0, concat_axis=0, tiled=True)
    grad_gate = call(
        home_kernel, jax.ShapeDtypeStruct((routes.shape[1], tokens), F32), [VMEM, VMEM], VMEM
    )(routes_t, back)
    return grad_pre.reshape(saved.shape), grad_gate.T


def solution(mesh):
    fine = Mesh(mesh.devices.reshape(2, 8, 4, 4, 2), ("zh", "y", "zl", "x", "c"))
    sp = ("zl", "x", "c")
    in_specs = (
        P(EP + sp, None),
        P(EP + sp, None),
        P(EP + sp, None),
        P(EP, sp, None, None),
        P(EP, None, sp),
    )
    out_specs = (P(EP, sp, None, None), P(EP + sp, None))
    return jax.shard_map(step, mesh=fine, in_specs=in_specs, out_specs=out_specs, check_vma=False)
```

```python
import functools

import jax
import jax.numpy as jnp
from jax import lax
from jax.experimental import pallas as pl
from jax.experimental.pallas import tpu as pltpu
from jax.sharding import Mesh, PartitionSpec as P


LANES = 128
CAPACITY = 16
STEP = 8
EP = ("zh", "y")
STAY, CROSS = 3, 4
F32, BF16 = jnp.float32, jnp.bfloat16
VMEM = pl.BlockSpec(memory_space=pltpu.VMEM)
SMEM = pl.BlockSpec(memory_space=pltpu.SMEM)


def ring(size, shift):
    return [((i + shift) % size, i) for i in range(size)]


def pack_kernel(core_ref, tokens_ref, routes_ref, keep_ref, send_ref):
    core = core_ref[0]
    rows = tokens_ref.shape[0]
    for ref, parity in ((keep_ref, core), (send_ref, 1 - core)):
        for b in range(ref.shape[1] // LANES):
            start = pl.multiple_of((2 * b + parity) * LANES, LANES)
            ref[:rows, b * LANES : (b + 1) * LANES] = tokens_ref[:, pl.ds(start, LANES)]
    send_ref[rows:, :] = jnp.zeros((send_ref.shape[0] - rows, send_ref.shape[1]), BF16)
    routes = routes_ref[...].astype(F32)
    send_ref[rows:, :LANES] = jnp.concatenate([routes, routes], axis=0).astype(BF16)


def places(routes, experts, first=0):
    tokens = routes.shape[1]
    wanted = (STEP * (lax.broadcasted_iota(jnp.int32, (experts, tokens), 0) + first)).astype(F32)
    hits = [routes[k : k + 1, :] == wanted for k in range(routes.shape[0])]
    member = functools.reduce(jnp.add, [h.astype(F32) for h in hits])
    before = lax.broadcasted_iota(jnp.int32, (tokens, tokens), 0) < lax.broadcasted_iota(
        jnp.int32, (tokens, tokens), 1
    )
    place = lax.dot_general(
        member.astype(BF16),
        before.astype(F32).astype(BF16),
        (((1,), (0,)), ((), ())),
        preferred_element_type=F32,
    )
    return hits, jnp.where(member > 0.5, place, -1.0)


def one_hot(place, capacity):
    experts, tokens = place.shape
    spread = jnp.broadcast_to(place[:, None, :], (experts, capacity, tokens))
    slot = lax.broadcasted_iota(jnp.int32, (experts, capacity, tokens), 1).astype(F32)
    return (spread == slot).astype(F32).reshape(experts * capacity, tokens)


def eye(shape):
    return lax.broadcasted_iota(jnp.int32, shape, 1) == lax.broadcasted_iota(jnp.int32, shape, 2)


def to_lanes(column, sources):
    rows = column.shape[0]
    shape = (sources, rows // sources, LANES)
    spread = jnp.broadcast_to(column, (rows, LANES)).reshape(shape)
    return jnp.sum(jnp.where(eye(shape), spread, 0.0), axis=1, keepdims=True)


def to_column(line, capacity):
    sources = line.shape[0]
    shape = (sources, capacity, LANES)
    spread = jnp.where(eye(shape), jnp.broadcast_to(line, shape), 0.0)
    return jnp.sum(spread.reshape(sources * capacity, LANES), axis=1, keepdims=True)


def send_rows(place, tokens_ref, out_ref, base):
    tokens = place.shape[1]
    experts, _, lanes = out_ref.shape
    chosen = one_hot(place, CAPACITY)
    rows = jnp.dot(chosen.astype(BF16), tokens_ref[:tokens, :], preferred_element_type=F32)
    rows = rows.astype(BF16)
    for b in range(rows.shape[1] // lanes):
        start = base + b * CAPACITY
        out_ref[:, start : start + CAPACITY, :] = rows[:, b * lanes : (b + 1) * lanes].reshape(
            experts, CAPACITY, lanes
        )
    return chosen


def dispatch_kernel(side, theirs, mine, info_ref, got_ref, keep_ref, routes_ref, gate_ref, out_ref):
    experts = out_ref.shape[0]
    first = info_ref[side] * experts
    height = got_ref.shape[1] // LANES * CAPACITY
    if theirs:
        table = got_ref[LANES:, :LANES].astype(F32)
        _, place = places(table[: table.shape[0] // 2], experts, first)
        send_rows(place, got_ref, out_ref, 0)
    if mine:
        base = height if theirs else 0
        gate = gate_ref[...].astype(F32)
        hits, place = places(routes_ref[...].astype(F32), experts, first)
        chosen = send_rows(place, keep_ref, out_ref, base)
        gates = functools.reduce(
            jnp.add, [jnp.where(h, gate[k : k + 1, :], 0.0) for k, h in enumerate(hits)]
        )
        spread = jnp.broadcast_to(gates[:, None, :], (experts, CAPACITY, gates.shape[1]))
        column = jnp.sum(chosen * spread.reshape(chosen.shape), axis=1, keepdims=True)
        line = to_lanes(column, experts)
        out_ref[:, base + height :, :] = jnp.broadcast_to(line, (experts, 8, LANES)).astype(BF16)


def take_rows(shifts, info_ref, sections, rows_ref):
    slots = rows_ref.shape[0] // len(sections)
    for m, (ref, base) in enumerate(sections):
        capacity = slots // ref.shape[0]
        for n, (dz, dx) in enumerate(shifts):
            chip = ((info_ref[1] + dz) & 3) * 4 + ((info_ref[2] + dx) & 3)
            start = pl.multiple_of(base + chip * capacity, capacity)
            rows_ref[m * slots : (m + 1) * slots, n * LANES : (n + 1) * LANES] = ref[
                :, pl.ds(start, capacity), :
            ].reshape(slots, LANES)


def theirs_kernel(shifts, info_ref, stay_ref, cross_ref, *refs):
    weights, (out_ref, whole_ref, rows_ref) = refs[:-3], refs[-3:]

    @pl.when(pl.program_id(0) == 0)
    def _():
        take_rows(shifts, info_ref, ((stay_ref, 0), (cross_ref, 0)), rows_ref)

    block = jnp.concatenate([w[i] for w in weights for i in range(w.shape[0])], axis=1)
    step = block.shape[0]
    whole_ref[pl.ds(pl.multiple_of(pl.program_id(0) * step, step), step), :] = block
    out_ref[...] = lax.dot_general(
        rows_ref[...], block, (((1,), (1,)), ((), ())), preferred_element_type=F32
    )


def mine_kernel(shifts, base, info_ref, stay_ref, cross_ref, whole_ref, out_ref, rows_ref):
    @pl.when(pl.program_id(0) == 0)
    def _():
        take_rows(shifts, info_ref, ((stay_ref, base), (cross_ref, 0)), rows_ref)

    step = out_ref.shape[1]
    block = whole_ref[pl.ds(pl.multiple_of(pl.program_id(0) * step, step), step), :]
    out_ref[...] = lax.dot_general(
        rows_ref[...], block, (((1,), (1,)), ((), ())), preferred_element_type=F32
    )


def piece(i, info):
    return ((i // 2) ^ info[STAY]) * 2 + i % 2


def finish_kernel(
    info_ref, mine_ref, theirs_ref, saved_ref, stay_ref, cross_ref, out_ref, score_ref
):
    rows, units = mine_ref.shape
    number = piece(pl.program_id(0), info_ref)
    here = pl.ds(pl.multiple_of(number * rows, rows), rows)
    sources = score_ref.shape[0]
    step = 256
    total = jnp.zeros((rows, 1), F32)
    line = jnp.where(number < 2, stay_ref[...].astype(F32), cross_ref[...].astype(F32))
    gate_in = to_column(line[:, :1, :], rows // sources)
    for j in range(units // step):
        cols = slice(j * step, (j + 1) * step)
        up_cols = slice(units + j * step, units + (j + 1) * step)
        grad = mine_ref[:, cols] + theirs_ref[here, cols]
        a = saved_ref[:, cols].astype(F32)
        u = saved_ref[:, up_cols].astype(F32)
        sig = 1.0 / (1.0 + jnp.exp(-a))
        silu = a * sig
        hidden = (silu * u).astype(BF16).astype(F32)
        total += jnp.sum(grad * hidden, axis=1, keepdims=True)
        scaled = grad * gate_in
        out_ref[:, cols] = (scaled * u * sig * (1.0 + a * (1.0 - sig))).astype(BF16)
        out_ref[:, up_cols] = (scaled * silu).astype(BF16)
    score_ref[...] = jnp.broadcast_to(to_lanes(total, sources), score_ref.shape)


def home_kernel(routes_ref, back_ref, out_ref):
    experts = back_ref.shape[0]
    routes = routes_ref[...].astype(F32)
    hits, place = places(routes, experts)
    chosen = one_hot(place, CAPACITY)
    column = to_column(back_ref[:, :1, :], CAPACITY)
    score = jnp.sum((column * chosen).reshape(experts, CAPACITY, -1), axis=1)
    for k, h in enumerate(hits):
        out_ref[k : k + 1, :] = jnp.sum(jnp.where(h, score, 0.0), axis=0, keepdims=True)


def call(kernel, shapes, in_specs, out_specs, scratch=(), grid=(), prefetch=0):
    return pl.pallas_call(
        kernel,
        out_shape=shapes,
        grid_spec=pltpu.PrefetchScalarGridSpec(
            num_scalar_prefetch=prefetch,
            grid=grid,
            in_specs=in_specs,
            out_specs=out_specs,
            scratch_shapes=list(scratch),
        ),
        compiler_params=pltpu.CompilerParams(vmem_limit_bytes=24 << 20),
    )


def near(array):
    return pltpu.with_memory_space_constraint(array, pltpu.VMEM)


def far(array):
    return pltpu.with_memory_space_constraint(array, pltpu.HBM)


def permute(array, axis, shift):
    return lax.ppermute(array, axis, ring(4, shift))


def gather_weights(block):
    z1, z3, z2 = (permute(block, "zl", r) for r in (1, 3, 2))
    trio = jnp.concatenate([block, z1, z3], axis=0)
    g1, g3 = permute(trio, "x", 1), permute(trio, "x", 3)
    h1, h3 = permute(z2, "x", 1), permute(z2, "x", 3)
    f1 = permute(g1[:2], "x", 1)
    f3 = permute(g3[2:], "x", 3)
    f2 = permute(h3, "x", 3)
    groups = [(trio, (0, 1, 3), 0), (g1, (0, 1, 3), 1), (g3, (0, 1, 3), 3)]
    groups += [(z2, (2,), 0), (h1, (2,), 1), (h3, (2,), 3)]
    return groups + [(f1, (0, 1), 2), (f3, (3,), 2), (f2, (2,), 2)]


def step(grad_out, routes, gate, saved, w_down):
    tokens, width = grad_out.shape
    units, slots = w_down.shape[1], saved.shape[2]
    sources = slots // CAPACITY
    groups = gather_weights(w_down)
    info = jnp.stack(
        [lax.axis_index(a) for a in ("c", "zl", "x", "zh")] + [1 - lax.axis_index("zh")]
    ).astype(jnp.int32)
    half = width // 2
    blocks = half // LANES
    routes_t, gate_t = routes.T, gate.T
    keep, send = call(
        pack_kernel,
        (
            jax.ShapeDtypeStruct((tokens, half), BF16),
            jax.ShapeDtypeStruct((tokens + 16, half), BF16),
        ),
        [SMEM, VMEM, VMEM],
        (VMEM, VMEM),
    )(info, far(grad_out), far(routes_t))
    got = lax.ppermute(send, "c", ring(2, 1))
    height = CAPACITY * blocks
    peers = sources // 2

    def along_y(side, theirs, mine):
        rows = height * (theirs + mine) + 8 * mine
        array = call(
            functools.partial(dispatch_kernel, side, theirs, mine),
            jax.ShapeDtypeStruct((peers, rows, LANES), BF16),
            [SMEM] + [VMEM] * 4,
            VMEM,
        )(info, got, keep, far(routes_t), far(gate_t))
        return lax.all_to_all(array, "y", split_axis=0, concat_axis=0, tiled=True)

    def across(array):
        return lax.ppermute(array, "zh", ring(2, 1))

    cross1 = across(along_y(CROSS, True, False))
    cross2 = across(along_y(CROSS, False, True))
    stay = along_y(STAY, True, True)
    part = 512
    columns = pl.BlockSpec((slots, part), lambda j: (0, j))
    shifts = [(dz, dx) for _, dzs, dx in groups for dz in dzs]
    arrays = [a for a, _, _ in groups]
    product = jax.ShapeDtypeStruct((slots, units), F32)
    scratch = [pltpu.VMEM((slots, half), BF16)]
    theirs, whole = call(
        functools.partial(theirs_kernel, shifts),
        (product, jax.ShapeDtypeStruct((units, half), BF16)),
        [SMEM, VMEM, VMEM]
        + [pl.BlockSpec((a.shape[0], part, LANES), lambda j: (0, j, 0)) for a in arrays],
        (columns, VMEM),
        scratch,
        (units // part,),
    )(info, near(stay), near(cross1), *map(far, arrays))
    theirs = lax.ppermute(theirs, "c", ring(2, 1))
    mine = call(
        functools.partial(mine_kernel, shifts, height),
        product,
        [SMEM, VMEM, VMEM, VMEM],
        columns,
        scratch,
        (units // part,),
    )(info, near(stay), near(cross2), near(whole))
    steps = 4
    rows = slots // steps
    tile = (sources // steps, 8, LANES)
    wide = pl.BlockSpec((rows, 2 * units), lambda i, info: (i, 0))
    gates = pl.BlockSpec(tile, lambda i, info: (i % 2, 0, 0))
    grad_pre, score = call(
        finish_kernel,
        (
            jax.ShapeDtypeStruct((slots, 2 * units), BF16),
            jax.ShapeDtypeStruct((sources, 8, LANES), F32),
        ),
        [pl.BlockSpec((rows, units), lambda i, info: (piece(i, info), 0)), VMEM, wide, gates, gates],
        (wide, pl.BlockSpec(tile, lambda i, info: (i, 0, 0))),
        grid=(steps,),
        prefetch=1,
    )(info, mine, near(theirs), saved[0, 0], stay[:, 2 * height :, :], cross2[:, height:, :])
    back = lax.all_to_all(score, EP, split_axis=0, concat_axis=0, tiled=True)
    grad_gate = call(
        home_kernel, jax.ShapeDtypeStruct((routes.shape[1], tokens), F32), [VMEM, VMEM], VMEM
    )(routes_t, back)
    return grad_pre.reshape(saved.shape), grad_gate.T


def solution(mesh):
    fine = Mesh(mesh.devices.reshape(2, 8, 4, 4, 2), ("zh", "y", "zl", "x", "c"))
    sp = ("zl", "x", "c")
    in_specs = (
        P(EP + sp, None),
        P(EP + sp, None),
        P(EP + sp, None),
        P(EP, sp, None, None),
        P(EP, None, sp),
    )
    out_specs = (P(EP, sp, None, None), P(EP + sp, None))
    return jax.shard_map(step, mesh=fine, in_specs=in_specs, out_specs=out_specs, check_vma=False)
```

```python
import functools

import jax
import jax.numpy as jnp
from jax import lax
from jax.experimental import pallas as pl
from jax.experimental.pallas import tpu as pltpu
from jax.sharding import Mesh, PartitionSpec as P


LANES = 128
CAPACITY = 16
STEP = 8
EP = ("zh", "y")
STAY, CROSS = 3, 4
F32, BF16 = jnp.float32, jnp.bfloat16
VMEM = pl.BlockSpec(memory_space=pltpu.VMEM)
SMEM = pl.BlockSpec(memory_space=pltpu.SMEM)


def ring(size, shift):
    return [((i + shift) % size, i) for i in range(size)]


def pack_kernel(core_ref, tokens_ref, routes_ref, keep_ref, send_ref):
    core = core_ref[0]
    rows = tokens_ref.shape[0]
    for ref, parity in ((keep_ref, core), (send_ref, 1 - core)):
        for b in range(ref.shape[1] // LANES):
            start = pl.multiple_of((2 * b + parity) * LANES, LANES)
            ref[:rows, b * LANES : (b + 1) * LANES] = tokens_ref[:, pl.ds(start, LANES)]
    send_ref[rows:, :] = jnp.zeros((send_ref.shape[0] - rows, send_ref.shape[1]), BF16)
    routes = routes_ref[...].astype(F32)
    send_ref[rows:, :LANES] = jnp.concatenate([routes, routes], axis=0).astype(BF16)


def places(routes, experts, first=0):
    tokens = routes.shape[1]
    wanted = (STEP * (lax.broadcasted_iota(jnp.int32, (experts, tokens), 0) + first)).astype(F32)
    hits = [routes[k : k + 1, :] == wanted for k in range(routes.shape[0])]
    member = functools.reduce(jnp.add, [h.astype(F32) for h in hits])
    before = lax.broadcasted_iota(jnp.int32, (tokens, tokens), 0) < lax.broadcasted_iota(
        jnp.int32, (tokens, tokens), 1
    )
    place = lax.dot_general(
        member.astype(BF16),
        before.astype(F32).astype(BF16),
        (((1,), (0,)), ((), ())),
        preferred_element_type=F32,
    )
    return hits, jnp.where(member > 0.5, place, -1.0)


def one_hot(place, capacity):
    experts, tokens = place.shape
    spread = jnp.broadcast_to(place[:, None, :], (experts, capacity, tokens))
    slot = lax.broadcasted_iota(jnp.int32, (experts, capacity, tokens), 1).astype(F32)
    return (spread == slot).astype(F32).reshape(experts * capacity, tokens)


def eye(shape):
    return lax.broadcasted_iota(jnp.int32, shape, 1) == lax.broadcasted_iota(jnp.int32, shape, 2)


def to_lanes(column, sources):
    rows = column.shape[0]
    shape = (sources, rows // sources, LANES)
    spread = jnp.broadcast_to(column, (rows, LANES)).reshape(shape)
    return jnp.sum(jnp.where(eye(shape), spread, 0.0), axis=1, keepdims=True)


def to_column(line, capacity):
    sources = line.shape[0]
    shape = (sources, capacity, LANES)
    spread = jnp.where(eye(shape), jnp.broadcast_to(line, shape), 0.0)
    return jnp.sum(spread.reshape(sources * capacity, LANES), axis=1, keepdims=True)


def send_rows(place, tokens_ref, out_ref, base):
    tokens = place.shape[1]
    experts, _, lanes = out_ref.shape
    chosen = one_hot(place, CAPACITY)
    rows = jnp.dot(chosen.astype(BF16), tokens_ref[:tokens, :], preferred_element_type=F32)
    rows = rows.astype(BF16)
    for b in range(rows.shape[1] // lanes):
        start = base + b * CAPACITY
        out_ref[:, start : start + CAPACITY, :] = rows[:, b * lanes : (b + 1) * lanes].reshape(
            experts, CAPACITY, lanes
        )
    return chosen


def dispatch_kernel(side, theirs, mine, info_ref, got_ref, keep_ref, routes_ref, gate_ref, out_ref):
    experts = out_ref.shape[0]
    first = info_ref[side] * experts
    height = got_ref.shape[1] // LANES * CAPACITY
    if theirs:
        table = got_ref[LANES:, :LANES].astype(F32)
        _, place = places(table[: table.shape[0] // 2], experts, first)
        send_rows(place, got_ref, out_ref, 0)
    if mine:
        base = height if theirs else 0
        gate = gate_ref[...].astype(F32)
        hits, place = places(routes_ref[...].astype(F32), experts, first)
        chosen = send_rows(place, keep_ref, out_ref, base)
        gates = functools.reduce(
            jnp.add, [jnp.where(h, gate[k : k + 1, :], 0.0) for k, h in enumerate(hits)]
        )
        spread = jnp.broadcast_to(gates[:, None, :], (experts, CAPACITY, gates.shape[1]))
        column = jnp.sum(chosen * spread.reshape(chosen.shape), axis=1, keepdims=True)
        line = to_lanes(column, experts)
        out_ref[:, base + height :, :] = jnp.broadcast_to(line, (experts, 8, LANES)).astype(BF16)


def take_rows(shifts, info_ref, sections, rows_ref):
    slots = rows_ref.shape[0] // len(sections)
    for m, (ref, base) in enumerate(sections):
        capacity = slots // ref.shape[0]
        for n, (dz, dx) in enumerate(shifts):
            chip = ((info_ref[1] + dz) & 3) * 4 + ((info_ref[2] + dx) & 3)
            start = pl.multiple_of(base + chip * capacity, capacity)
            rows_ref[m * slots : (m + 1) * slots, n * LANES : (n + 1) * LANES] = ref[
                :, pl.ds(start, capacity), :
            ].reshape(slots, LANES)


def theirs_kernel(shifts, info_ref, stay_ref, cross_ref, *refs):
    weights, (out_ref, whole_ref, rows_ref) = refs[:-3], refs[-3:]

    @pl.when(pl.program_id(0) == 0)
    def _():
        take_rows(shifts, info_ref, ((stay_ref, 0), (cross_ref, 0)), rows_ref)

    block = jnp.concatenate([w[i] for w in weights for i in range(w.shape[0])], axis=1)
    step = block.shape[0]
    whole_ref[pl.ds(pl.multiple_of(pl.program_id(0) * step, step), step), :] = block
    out_ref[...] = lax.dot_general(
        rows_ref[...], block, (((1,), (1,)), ((), ())), preferred_element_type=F32
    )


def mine_kernel(shifts, base, info_ref, stay_ref, cross_ref, whole_ref, out_ref, rows_ref):
    @pl.when(pl.program_id(0) == 0)
    def _():
        take_rows(shifts, info_ref, ((stay_ref, base), (cross_ref, 0)), rows_ref)

    step = out_ref.shape[1]
    block = whole_ref[pl.ds(pl.multiple_of(pl.program_id(0) * step, step), step), :]
    out_ref[...] = lax.dot_general(
        rows_ref[...], block, (((1,), (1,)), ((), ())), preferred_element_type=F32
    )


def piece(i, info):
    return ((i // 2) ^ info[STAY]) * 2 + i % 2


def finish_kernel(
    info_ref, mine_ref, theirs_ref, saved_ref, stay_ref, cross_ref, out_ref, score_ref
):
    rows, units = mine_ref.shape
    number = piece(pl.program_id(0), info_ref)
    here = pl.ds(pl.multiple_of(number * rows, rows), rows)
    sources = score_ref.shape[0]
    step = 256
    total = jnp.zeros((rows, 1), F32)
    line = jnp.where(number < 2, stay_ref[...].astype(F32), cross_ref[...].astype(F32))
    gate_in = to_column(line[:, :1, :], rows // sources)
    for j in range(units // step):
        cols = slice(j * step, (j + 1) * step)
        up_cols = slice(units + j * step, units + (j + 1) * step)
        grad = mine_ref[:, cols] + theirs_ref[here, cols]
        a = saved_ref[:, cols].astype(F32)
        u = saved_ref[:, up_cols].astype(F32)
        sig = 1.0 / (1.0 + jnp.exp(-a))
        silu = a * sig
        hidden = (silu * u).astype(BF16).astype(F32)
        total += jnp.sum(grad * hidden, axis=1, keepdims=True)
        scaled = grad * gate_in
        out_ref[:, cols] = (scaled * u * sig * (1.0 + a * (1.0 - sig))).astype(BF16)
        out_ref[:, up_cols] = (scaled * silu).astype(BF16)
    score_ref[...] = jnp.broadcast_to(to_lanes(total, sources), score_ref.shape)


def home_kernel(routes_ref, back_ref, out_ref):
    experts = back_ref.shape[0]
    routes = routes_ref[...].astype(F32)
    hits, place = places(routes, experts)
    chosen = one_hot(place, CAPACITY)
    column = to_column(back_ref[:, :1, :], CAPACITY)
    score = jnp.sum((column * chosen).reshape(experts, CAPACITY, -1), axis=1)
    for k, h in enumerate(hits):
        out_ref[k : k + 1, :] = jnp.sum(jnp.where(h, score, 0.0), axis=0, keepdims=True)


def call(kernel, shapes, in_specs, out_specs, scratch=(), grid=(), prefetch=0):
    return pl.pallas_call(
        kernel,
        out_shape=shapes,
        grid_spec=pltpu.PrefetchScalarGridSpec(
            num_scalar_prefetch=prefetch,
            grid=grid,
            in_specs=in_specs,
            out_specs=out_specs,
            scratch_shapes=list(scratch),
        ),
        compiler_params=pltpu.CompilerParams(vmem_limit_bytes=24 << 20),
    )


def near(array):
    return pltpu.with_memory_space_constraint(array, pltpu.VMEM)


def far(array):
    return pltpu.with_memory_space_constraint(array, pltpu.HBM)


def permute(array, axis, shift):
    return lax.ppermute(array, axis, ring(4, shift))


def gather_weights(block):
    z1, z3, z2 = (permute(block, "zl", r) for r in (1, 3, 2))
    trio = jnp.concatenate([block, z1, z3], axis=0)
    g1, g3 = permute(trio, "x", 1), permute(trio, "x", 3)
    e2 = permute(z2, "x", 2)
    f1 = permute(jnp.concatenate([g1[:2], z2], axis=0), "x", 1)
    f3 = permute(jnp.concatenate([g3[2:], z2], axis=0), "x", 3)
    groups = [(a, [(dz, dx) for dz in (0, 1, 3)]) for a, dx in ((trio, 0), (g1, 1), (g3, 3))]
    groups += [(z2, [(2, 0)]), (e2, [(2, 2)])]
    return groups + [(f1, [(0, 2), (1, 2), (2, 1)]), (f3, [(3, 2), (2, 3)])]


def step(grad_out, routes, gate, saved, w_down):
    tokens, width = grad_out.shape
    units, slots = w_down.shape[1], saved.shape[2]
    sources = slots // CAPACITY
    groups = gather_weights(w_down)
    info = jnp.stack(
        [lax.axis_index(a) for a in ("c", "zl", "x", "zh")] + [1 - lax.axis_index("zh")]
    ).astype(jnp.int32)
    half = width // 2
    blocks = half // LANES
    routes_t, gate_t = routes.T, gate.T
    keep, send = call(
        pack_kernel,
        (
            jax.ShapeDtypeStruct((tokens, half), BF16),
            jax.ShapeDtypeStruct((tokens + 16, half), BF16),
        ),
        [SMEM, VMEM, VMEM],
        (VMEM, VMEM),
    )(info, far(grad_out), far(routes_t))
    got = lax.ppermute(send, "c", ring(2, 1))
    height = CAPACITY * blocks
    peers = sources // 2

    def along_y(side, theirs, mine):
        rows = height * (theirs + mine) + 8 * mine
        array = call(
            functools.partial(dispatch_kernel, side, theirs, mine),
            jax.ShapeDtypeStruct((peers, rows, LANES), BF16),
            [SMEM] + [VMEM] * 4,
            VMEM,
        )(info, got, keep, far(routes_t), far(gate_t))
        return lax.all_to_all(array, "y", split_axis=0, concat_axis=0, tiled=True)

    def across(array):
        return lax.ppermute(array, "zh", ring(2, 1))

    cross1 = across(along_y(CROSS, True, False))
    cross2 = across(along_y(CROSS, False, True))
    stay = along_y(STAY, True, True)
    part = 512
    columns = pl.BlockSpec((slots, part), lambda j: (0, j))
    shifts = [pair for _, pairs in groups for pair in pairs]
    arrays = [a for a, _ in groups]
    product = jax.ShapeDtypeStruct((slots, units), F32)
    scratch = [pltpu.VMEM((slots, half), BF16)]
    theirs, whole = call(
        functools.partial(theirs_kernel, shifts),
        (product, jax.ShapeDtypeStruct((units, half), BF16)),
        [SMEM, VMEM, VMEM]
        + [pl.BlockSpec((a.shape[0], part, LANES), lambda j: (0, j, 0)) for a in arrays],
        (columns, VMEM),
        scratch,
        (units // part,),
    )(info, near(stay), near(cross1), *map(far, arrays))
    theirs = lax.ppermute(theirs, "c", ring(2, 1))
    mine = call(
        functools.partial(mine_kernel, shifts, height),
        product,
        [SMEM, VMEM, VMEM, VMEM],
        columns,
        scratch,
        (units // part,),
    )(info, near(stay), near(cross2), near(whole))
    steps = 4
    rows = slots // steps
    tile = (sources // steps, 8, LANES)
    wide = pl.BlockSpec((rows, 2 * units), lambda i, info: (i, 0))
    gates = pl.BlockSpec(tile, lambda i, info: (i % 2, 0, 0))
    grad_pre, score = call(
        finish_kernel,
        (
            jax.ShapeDtypeStruct((slots, 2 * units), BF16),
            jax.ShapeDtypeStruct((sources, 8, LANES), F32),
        ),
        [pl.BlockSpec((rows, units), lambda i, info: (piece(i, info), 0)), VMEM, wide, gates, gates],
        (wide, pl.BlockSpec(tile, lambda i, info: (i, 0, 0))),
        grid=(steps,),
        prefetch=1,
    )(info, mine, near(theirs), saved[0, 0], stay[:, 2 * height :, :], cross2[:, height:, :])
    back = lax.all_to_all(score, EP, split_axis=0, concat_axis=0, tiled=True)
    grad_gate = call(
        home_kernel, jax.ShapeDtypeStruct((routes.shape[1], tokens), F32), [VMEM, VMEM], VMEM
    )(routes_t, back)
    return grad_pre.reshape(saved.shape), grad_gate.T


def solution(mesh):
    fine = Mesh(mesh.devices.reshape(2, 8, 4, 4, 2), ("zh", "y", "zl", "x", "c"))
    sp = ("zl", "x", "c")
    in_specs = (
        P(EP + sp, None),
        P(EP + sp, None),
        P(EP + sp, None),
        P(EP, sp, None, None),
        P(EP, None, sp),
    )
    out_specs = (P(EP, sp, None, None), P(EP + sp, None))
    return jax.shard_map(step, mesh=fine, in_specs=in_specs, out_specs=out_specs, check_vma=False)
```

```python
import functools

import jax
import jax.numpy as jnp
from jax import lax
from jax.experimental import pallas as pl
from jax.experimental.pallas import tpu as pltpu
from jax.sharding import Mesh, PartitionSpec as P


LANES = 128
CAPACITY = 16
STEP = 8
EP = ("zh", "y")
STAY, CROSS = 3, 4
F32, BF16 = jnp.float32, jnp.bfloat16
VMEM = pl.BlockSpec(memory_space=pltpu.VMEM)
SMEM = pl.BlockSpec(memory_space=pltpu.SMEM)


def ring(size, shift):
    return [((i + shift) % size, i) for i in range(size)]


def pack_kernel(core_ref, tokens_ref, routes_ref, keep_ref, send_ref):
    core = core_ref[0]
    rows = tokens_ref.shape[0]
    for ref, parity in ((keep_ref, core), (send_ref, 1 - core)):
        for b in range(ref.shape[1] // LANES):
            start = pl.multiple_of((2 * b + parity) * LANES, LANES)
            ref[:rows, b * LANES : (b + 1) * LANES] = tokens_ref[:, pl.ds(start, LANES)]
    send_ref[rows:, :] = jnp.zeros((send_ref.shape[0] - rows, send_ref.shape[1]), BF16)
    routes = routes_ref[...].astype(F32)
    send_ref[rows:, :LANES] = jnp.concatenate([routes, routes], axis=0).astype(BF16)


def places(routes, experts, first=0):
    tokens = routes.shape[1]
    wanted = (STEP * (lax.broadcasted_iota(jnp.int32, (experts, tokens), 0) + first)).astype(F32)
    hits = [routes[k : k + 1, :] == wanted for k in range(routes.shape[0])]
    member = functools.reduce(jnp.add, [h.astype(F32) for h in hits])
    before = lax.broadcasted_iota(jnp.int32, (tokens, tokens), 0) < lax.broadcasted_iota(
        jnp.int32, (tokens, tokens), 1
    )
    place = lax.dot_general(
        member.astype(BF16),
        before.astype(F32).astype(BF16),
        (((1,), (0,)), ((), ())),
        preferred_element_type=F32,
    )
    return hits, jnp.where(member > 0.5, place, -1.0)


def one_hot(place, capacity):
    experts, tokens = place.shape
    spread = jnp.broadcast_to(place[:, None, :], (experts, capacity, tokens))
    slot = lax.broadcasted_iota(jnp.int32, (experts, capacity, tokens), 1).astype(F32)
    return (spread == slot).astype(F32).reshape(experts * capacity, tokens)


def eye(shape):
    return lax.broadcasted_iota(jnp.int32, shape, 1) == lax.broadcasted_iota(jnp.int32, shape, 2)


def to_lanes(column, sources):
    rows = column.shape[0]
    shape = (sources, rows // sources, LANES)
    spread = jnp.broadcast_to(column, (rows, LANES)).reshape(shape)
    return jnp.sum(jnp.where(eye(shape), spread, 0.0), axis=1, keepdims=True)


def to_column(line, capacity):
    sources = line.shape[0]
    shape = (sources, capacity, LANES)
    spread = jnp.where(eye(shape), jnp.broadcast_to(line, shape), 0.0)
    return jnp.sum(spread.reshape(sources * capacity, LANES), axis=1, keepdims=True)


def send_rows(place, tokens_ref, out_ref, base):
    tokens = place.shape[1]
    experts, _, lanes = out_ref.shape
    chosen = one_hot(place, CAPACITY)
    rows = jnp.dot(chosen.astype(BF16), tokens_ref[:tokens, :], preferred_element_type=F32)
    rows = rows.astype(BF16)
    for b in range(rows.shape[1] // lanes):
        start = base + b * CAPACITY
        out_ref[:, start : start + CAPACITY, :] = rows[:, b * lanes : (b + 1) * lanes].reshape(
            experts, CAPACITY, lanes
        )
    return chosen


def dispatch_kernel(side, theirs, mine, info_ref, got_ref, keep_ref, routes_ref, gate_ref, out_ref):
    experts = out_ref.shape[0]
    first = info_ref[side] * experts
    height = got_ref.shape[1] // LANES * CAPACITY
    if theirs:
        table = got_ref[LANES:, :LANES].astype(F32)
        _, place = places(table[: table.shape[0] // 2], experts, first)
        send_rows(place, got_ref, out_ref, 0)
    if mine:
        base = height if theirs else 0
        gate = gate_ref[...].astype(F32)
        hits, place = places(routes_ref[...].astype(F32), experts, first)
        chosen = send_rows(place, keep_ref, out_ref, base)
        gates = functools.reduce(
            jnp.add, [jnp.where(h, gate[k : k + 1, :], 0.0) for k, h in enumerate(hits)]
        )
        spread = jnp.broadcast_to(gates[:, None, :], (experts, CAPACITY, gates.shape[1]))
        column = jnp.sum(chosen * spread.reshape(chosen.shape), axis=1, keepdims=True)
        line = to_lanes(column, experts)
        out_ref[:, base + height :, :] = jnp.broadcast_to(line, (experts, 8, LANES)).astype(BF16)


def take_rows(shifts, info_ref, sections, rows_ref):
    slots = rows_ref.shape[0] // len(sections)
    for m, (ref, base) in enumerate(sections):
        capacity = slots // ref.shape[0]
        for n, (dz, dx) in enumerate(shifts):
            chip = ((info_ref[1] + dz) & 3) * 4 + ((info_ref[2] + dx) & 3)
            start = pl.multiple_of(base + chip * capacity, capacity)
            rows_ref[m * slots : (m + 1) * slots, n * LANES : (n + 1) * LANES] = ref[
                :, pl.ds(start, capacity), :
            ].reshape(slots, LANES)


def theirs_kernel(shifts, info_ref, stay_ref, cross_ref, *refs):
    weights, (out_ref, whole_ref, rows_ref) = refs[:-3], refs[-3:]

    @pl.when(pl.program_id(0) == 0)
    def _():
        take_rows(shifts, info_ref, ((stay_ref, 0), (cross_ref, 0)), rows_ref)

    block = jnp.concatenate([w[i] for w in weights for i in range(w.shape[0])], axis=1)
    step = block.shape[0]
    whole_ref[pl.ds(pl.multiple_of(pl.program_id(0) * step, step), step), :] = block
    out_ref[...] = lax.dot_general(
        rows_ref[...], block, (((1,), (1,)), ((), ())), preferred_element_type=F32
    )


def mine_kernel(shifts, base, info_ref, stay_ref, cross_ref, whole_ref, out_ref, rows_ref):
    @pl.when(pl.program_id(0) == 0)
    def _():
        take_rows(shifts, info_ref, ((stay_ref, base), (cross_ref, 0)), rows_ref)

    step = out_ref.shape[1]
    block = whole_ref[pl.ds(pl.multiple_of(pl.program_id(0) * step, step), step), :]
    out_ref[...] = lax.dot_general(
        rows_ref[...], block, (((1,), (1,)), ((), ())), preferred_element_type=F32
    )


def piece(i, info):
    return ((i // 2) ^ info[STAY]) * 2 + i % 2


def finish_kernel(
    info_ref, mine_ref, theirs_ref, saved_ref, stay_ref, cross_ref, out_ref, score_ref
):
    rows, units = mine_ref.shape
    number = piece(pl.program_id(0), info_ref)
    here = pl.ds(pl.multiple_of(number * rows, rows), rows)
    sources = score_ref.shape[0]
    step = 256
    total = jnp.zeros((rows, 1), F32)
    line = jnp.where(number < 2, stay_ref[...].astype(F32), cross_ref[...].astype(F32))
    gate_in = to_column(line[:, :1, :], rows // sources)
    for j in range(units // step):
        cols = slice(j * step, (j + 1) * step)
        up_cols = slice(units + j * step, units + (j + 1) * step)
        grad = mine_ref[:, cols] + theirs_ref[here, cols]
        a = saved_ref[:, cols].astype(F32)
        u = saved_ref[:, up_cols].astype(F32)
        sig = 1.0 / (1.0 + jnp.exp(-a))
        silu = a * sig
        hidden = (silu * u).astype(BF16).astype(F32)
        total += jnp.sum(grad * hidden, axis=1, keepdims=True)
        scaled = grad * gate_in
        out_ref[:, cols] = (scaled * u * sig * (1.0 + a * (1.0 - sig))).astype(BF16)
        out_ref[:, up_cols] = (scaled * silu).astype(BF16)
    score_ref[...] = jnp.broadcast_to(to_lanes(total, sources), score_ref.shape)


def home_kernel(routes_ref, back_ref, out_ref):
    experts = back_ref.shape[0]
    routes = routes_ref[...].astype(F32)
    hits, place = places(routes, experts)
    chosen = one_hot(place, CAPACITY)
    column = to_column(back_ref[:, :1, :], CAPACITY)
    score = jnp.sum((column * chosen).reshape(experts, CAPACITY, -1), axis=1)
    for k, h in enumerate(hits):
        out_ref[k : k + 1, :] = jnp.sum(jnp.where(h, score, 0.0), axis=0, keepdims=True)


def call(kernel, shapes, in_specs, out_specs, scratch=(), grid=(), prefetch=0):
    return pl.pallas_call(
        kernel,
        out_shape=shapes,
        grid_spec=pltpu.PrefetchScalarGridSpec(
            num_scalar_prefetch=prefetch,
            grid=grid,
            in_specs=in_specs,
            out_specs=out_specs,
            scratch_shapes=list(scratch),
        ),
        compiler_params=pltpu.CompilerParams(vmem_limit_bytes=24 << 20),
    )


def near(array):
    return pltpu.with_memory_space_constraint(array, pltpu.VMEM)


def far(array):
    return pltpu.with_memory_space_constraint(array, pltpu.HBM)


def permute(array, axis, shift):
    return lax.ppermute(array, axis, ring(4, shift))


def gather_weights(block):
    z1, z3, z2 = (permute(block, "zl", r) for r in (1, 3, 2))
    a2 = permute(block, "x", 2)
    trio = jnp.concatenate([block, z1, z3], axis=0)
    g1, g3 = permute(trio, "x", 1), permute(trio, "x", 3)
    h1, h3, e2 = permute(z2, "x", 1), permute(z2, "x", 3), permute(z2, "x", 2)
    from_up, from_down = g1[1:2], g3[2:]
    f1, f3 = permute(from_up, "x", 1), permute(from_down, "x", 3)
    groups = [(a, [(dz, dx) for dz in (0, 1, 3)]) for a, dx in ((trio, 0), (g1, 1), (g3, 3))]
    groups += [(a, [(2, dx)]) for a, dx in ((z2, 0), (h1, 1), (h3, 3), (e2, 2))]
    return groups + [(a2, [(0, 2)]), (f1, [(1, 2)]), (f3, [(3, 2)])]


def step(grad_out, routes, gate, saved, w_down):
    tokens, width = grad_out.shape
    units, slots = w_down.shape[1], saved.shape[2]
    sources = slots // CAPACITY
    groups = gather_weights(w_down)
    info = jnp.stack(
        [lax.axis_index(a) for a in ("c", "zl", "x", "zh")] + [1 - lax.axis_index("zh")]
    ).astype(jnp.int32)
    half = width // 2
    blocks = half // LANES
    routes_t, gate_t = routes.T, gate.T
    keep, send = call(
        pack_kernel,
        (
            jax.ShapeDtypeStruct((tokens, half), BF16),
            jax.ShapeDtypeStruct((tokens + 16, half), BF16),
        ),
        [SMEM, VMEM, VMEM],
        (VMEM, VMEM),
    )(info, far(grad_out), far(routes_t))
    got = lax.ppermute(send, "c", ring(2, 1))
    height = CAPACITY * blocks
    peers = sources // 2

    def along_y(side, theirs, mine):
        rows = height * (theirs + mine) + 8 * mine
        array = call(
            functools.partial(dispatch_kernel, side, theirs, mine),
            jax.ShapeDtypeStruct((peers, rows, LANES), BF16),
            [SMEM] + [VMEM] * 4,
            VMEM,
        )(info, got, keep, far(routes_t), far(gate_t))
        return lax.all_to_all(array, "y", split_axis=0, concat_axis=0, tiled=True)

    def across(array):
        return lax.ppermute(array, "zh", ring(2, 1))

    cross1 = across(along_y(CROSS, True, False))
    cross2 = across(along_y(CROSS, False, True))
    stay = along_y(STAY, True, True)
    part = 512
    columns = pl.BlockSpec((slots, part), lambda j: (0, j))
    shifts = [pair for _, pairs in groups for pair in pairs]
    arrays = [a for a, _ in groups]
    product = jax.ShapeDtypeStruct((slots, units), F32)
    scratch = [pltpu.VMEM((slots, half), BF16)]
    theirs, whole = call(
        functools.partial(theirs_kernel, shifts),
        (product, jax.ShapeDtypeStruct((units, half), BF16)),
        [SMEM, VMEM, VMEM]
        + [pl.BlockSpec((a.shape[0], part, LANES), lambda j: (0, j, 0)) for a in arrays],
        (columns, VMEM),
        scratch,
        (units // part,),
    )(info, near(stay), near(cross1), *map(far, arrays))
    theirs = lax.ppermute(theirs, "c", ring(2, 1))
    mine = call(
        functools.partial(mine_kernel, shifts, height),
        product,
        [SMEM, VMEM, VMEM, VMEM],
        columns,
        scratch,
        (units // part,),
    )(info, near(stay), near(cross2), near(whole))
    steps = 4
    rows = slots // steps
    tile = (sources // steps, 8, LANES)
    wide = pl.BlockSpec((rows, 2 * units), lambda i, info: (i, 0))
    gates = pl.BlockSpec(tile, lambda i, info: (i % 2, 0, 0))
    grad_pre, score = call(
        finish_kernel,
        (
            jax.ShapeDtypeStruct((slots, 2 * units), BF16),
            jax.ShapeDtypeStruct((sources, 8, LANES), F32),
        ),
        [pl.BlockSpec((rows, units), lambda i, info: (piece(i, info), 0)), VMEM, wide, gates, gates],
        (wide, pl.BlockSpec(tile, lambda i, info: (i, 0, 0))),
        grid=(steps,),
        prefetch=1,
    )(info, mine, near(theirs), saved[0, 0], stay[:, 2 * height :, :], cross2[:, height:, :])
    back = lax.all_to_all(score, EP, split_axis=0, concat_axis=0, tiled=True)
    grad_gate = call(
        home_kernel, jax.ShapeDtypeStruct((routes.shape[1], tokens), F32), [VMEM, VMEM], VMEM
    )(routes_t, back)
    return grad_pre.reshape(saved.shape), grad_gate.T


def solution(mesh):
    fine = Mesh(mesh.devices.reshape(2, 8, 4, 4, 2), ("zh", "y", "zl", "x", "c"))
    sp = ("zl", "x", "c")
    in_specs = (
        P(EP + sp, None),
        P(EP + sp, None),
        P(EP + sp, None),
        P(EP, sp, None, None),
        P(EP, None, sp),
    )
    out_specs = (P(EP, sp, None, None), P(EP + sp, None))
    return jax.shard_map(step, mesh=fine, in_specs=in_specs, out_specs=out_specs, check_vma=False)
```

```python
import functools

import jax
import jax.numpy as jnp
from jax import lax
from jax.experimental import pallas as pl
from jax.experimental.pallas import tpu as pltpu
from jax.sharding import Mesh, PartitionSpec as P


LANES = 128
CAPACITY = 16
STEP = 8
EP = ("zh", "y")
STAY, CROSS = 3, 4
F32, BF16 = jnp.float32, jnp.bfloat16
VMEM = pl.BlockSpec(memory_space=pltpu.VMEM)
SMEM = pl.BlockSpec(memory_space=pltpu.SMEM)


def ring(size, shift):
    return [((i + shift) % size, i) for i in range(size)]


def pack_kernel(core_ref, tokens_ref, routes_ref, keep_ref, send_ref):
    core = core_ref[0]
    rows = tokens_ref.shape[0]
    for ref, parity in ((keep_ref, core), (send_ref, 1 - core)):
        for b in range(ref.shape[1] // LANES):
            start = pl.multiple_of((2 * b + parity) * LANES, LANES)
            ref[:rows, b * LANES : (b + 1) * LANES] = tokens_ref[:, pl.ds(start, LANES)]
    send_ref[rows:, :] = jnp.zeros((send_ref.shape[0] - rows, send_ref.shape[1]), BF16)
    routes = routes_ref[...].astype(F32)
    send_ref[rows:, :LANES] = jnp.concatenate([routes, routes], axis=0).astype(BF16)


def places(routes, experts, first=0):
    tokens = routes.shape[1]
    wanted = (STEP * (lax.broadcasted_iota(jnp.int32, (experts, tokens), 0) + first)).astype(F32)
    hits = [routes[k : k + 1, :] == wanted for k in range(routes.shape[0])]
    member = functools.reduce(jnp.add, [h.astype(F32) for h in hits])
    before = lax.broadcasted_iota(jnp.int32, (tokens, tokens), 0) < lax.broadcasted_iota(
        jnp.int32, (tokens, tokens), 1
    )
    place = lax.dot_general(
        member.astype(BF16),
        before.astype(F32).astype(BF16),
        (((1,), (0,)), ((), ())),
        preferred_element_type=F32,
    )
    return hits, jnp.where(member > 0.5, place, -1.0)


def one_hot(place, capacity):
    experts, tokens = place.shape
    spread = jnp.broadcast_to(place[:, None, :], (experts, capacity, tokens))
    slot = lax.broadcasted_iota(jnp.int32, (experts, capacity, tokens), 1).astype(F32)
    return (spread == slot).astype(F32).reshape(experts * capacity, tokens)


def eye(shape):
    return lax.broadcasted_iota(jnp.int32, shape, 1) == lax.broadcasted_iota(jnp.int32, shape, 2)


def to_lanes(column, sources):
    rows = column.shape[0]
    shape = (sources, rows // sources, LANES)
    spread = jnp.broadcast_to(column, (rows, LANES)).reshape(shape)
    return jnp.sum(jnp.where(eye(shape), spread, 0.0), axis=1, keepdims=True)


def to_column(line, capacity):
    sources = line.shape[0]
    shape = (sources, capacity, LANES)
    spread = jnp.where(eye(shape), jnp.broadcast_to(line, shape), 0.0)
    return jnp.sum(spread.reshape(sources * capacity, LANES), axis=1, keepdims=True)


def send_rows(place, tokens_ref, out_ref, base):
    tokens = place.shape[1]
    experts, _, lanes = out_ref.shape
    chosen = one_hot(place, CAPACITY)
    rows = jnp.dot(chosen.astype(BF16), tokens_ref[:tokens, :], preferred_element_type=F32)
    rows = rows.astype(BF16)
    for b in range(rows.shape[1] // lanes):
        start = base + b * CAPACITY
        out_ref[:, start : start + CAPACITY, :] = rows[:, b * lanes : (b + 1) * lanes].reshape(
            experts, CAPACITY, lanes
        )
    return chosen


def dispatch_kernel(side, theirs, mine, info_ref, got_ref, keep_ref, routes_ref, gate_ref, out_ref):
    experts = out_ref.shape[0]
    first = info_ref[side] * experts
    height = got_ref.shape[1] // LANES * CAPACITY
    if theirs:
        table = got_ref[LANES:, :LANES].astype(F32)
        _, place = places(table[: table.shape[0] // 2], experts, first)
        send_rows(place, got_ref, out_ref, 0)
    if mine:
        base = height if theirs else 0
        gate = gate_ref[...].astype(F32)
        hits, place = places(routes_ref[...].astype(F32), experts, first)
        chosen = send_rows(place, keep_ref, out_ref, base)
        gates = functools.reduce(
            jnp.add, [jnp.where(h, gate[k : k + 1, :], 0.0) for k, h in enumerate(hits)]
        )
        spread = jnp.broadcast_to(gates[:, None, :], (experts, CAPACITY, gates.shape[1]))
        column = jnp.sum(chosen * spread.reshape(chosen.shape), axis=1, keepdims=True)
        line = to_lanes(column, experts)
        out_ref[:, base + height :, :] = jnp.broadcast_to(line, (experts, 8, LANES)).astype(BF16)


def take_rows(shifts, info_ref, sections, rows_ref):
    slots = rows_ref.shape[0] // len(sections)
    for m, (ref, base) in enumerate(sections):
        capacity = slots // ref.shape[0]
        for n, (dz, dx) in enumerate(shifts):
            chip = ((info_ref[1] + dz) & 3) * 4 + ((info_ref[2] + dx) & 3)
            start = pl.multiple_of(base + chip * capacity, capacity)
            rows_ref[m * slots : (m + 1) * slots, n * LANES : (n + 1) * LANES] = ref[
                :, pl.ds(start, capacity), :
            ].reshape(slots, LANES)


def theirs_kernel(shifts, info_ref, stay_ref, cross_ref, *refs):
    weights, (out_ref, whole_ref, rows_ref) = refs[:-3], refs[-3:]

    @pl.when(pl.program_id(0) == 0)
    def _():
        take_rows(shifts, info_ref, ((stay_ref, 0), (cross_ref, 0)), rows_ref)

    block = jnp.concatenate([w[i] for w in weights for i in range(w.shape[0])], axis=1)
    step = block.shape[0]
    whole_ref[pl.ds(pl.multiple_of(pl.program_id(0) * step, step), step), :] = block
    out_ref[...] = lax.dot_general(
        rows_ref[...], block, (((1,), (1,)), ((), ())), preferred_element_type=F32
    )


def mine_kernel(shifts, base, info_ref, stay_ref, cross_ref, whole_ref, out_ref, rows_ref):
    @pl.when(pl.program_id(0) == 0)
    def _():
        take_rows(shifts, info_ref, ((stay_ref, base), (cross_ref, 0)), rows_ref)

    step = out_ref.shape[1]
    block = whole_ref[pl.ds(pl.multiple_of(pl.program_id(0) * step, step), step), :]
    out_ref[...] = lax.dot_general(
        rows_ref[...], block, (((1,), (1,)), ((), ())), preferred_element_type=F32
    )


def piece(i, info):
    return ((i // 2) ^ info[STAY]) * 2 + i % 2


def slopes_kernel(saved_ref, gate_slope_ref, up_slope_ref, hidden_ref):
    units = hidden_ref.shape[1]
    step = 256
    for j in range(units // step):
        cols = slice(j * step, (j + 1) * step)
        a = saved_ref[:, cols].astype(F32)
        u = saved_ref[:, units + j * step : units + (j + 1) * step].astype(F32)
        sig = 1.0 / (1.0 + jnp.exp(-a))
        silu = a * sig
        hidden_ref[:, cols] = (silu * u).astype(BF16)
        gate_slope_ref[:, cols] = u * sig * (1.0 + a * (1.0 - sig))
        up_slope_ref[:, cols] = silu


def finish_kernel(
    info_ref,
    mine_ref,
    theirs_ref,
    gate_slope_ref,
    up_slope_ref,
    hidden_ref,
    stay_ref,
    cross_ref,
    out_ref,
    score_ref,
):
    rows, units = mine_ref.shape
    number = piece(pl.program_id(0), info_ref)
    here = pl.ds(pl.multiple_of(number * rows, rows), rows)
    sources = score_ref.shape[0]
    step = 256
    total = jnp.zeros((rows, 1), F32)
    line = jnp.where(number < 2, stay_ref[...].astype(F32), cross_ref[...].astype(F32))
    gate_in = to_column(line[:, :1, :], rows // sources)
    for j in range(units // step):
        cols = slice(j * step, (j + 1) * step)
        up_cols = slice(units + j * step, units + (j + 1) * step)
        grad = mine_ref[:, cols] + theirs_ref[here, cols]
        total += jnp.sum(grad * hidden_ref[:, cols].astype(F32), axis=1, keepdims=True)
        scaled = grad * gate_in
        out_ref[:, cols] = (scaled * gate_slope_ref[:, cols]).astype(BF16)
        out_ref[:, up_cols] = (scaled * up_slope_ref[:, cols]).astype(BF16)
    score_ref[...] = jnp.broadcast_to(to_lanes(total, sources), score_ref.shape)


def home_kernel(routes_ref, back_ref, out_ref):
    experts = back_ref.shape[0]
    routes = routes_ref[...].astype(F32)
    hits, place = places(routes, experts)
    chosen = one_hot(place, CAPACITY)
    column = to_column(back_ref[:, :1, :], CAPACITY)
    score = jnp.sum((column * chosen).reshape(experts, CAPACITY, -1), axis=1)
    for k, h in enumerate(hits):
        out_ref[k : k + 1, :] = jnp.sum(jnp.where(h, score, 0.0), axis=0, keepdims=True)


def call(kernel, shapes, in_specs, out_specs, scratch=(), grid=(), prefetch=0):
    return pl.pallas_call(
        kernel,
        out_shape=shapes,
        grid_spec=pltpu.PrefetchScalarGridSpec(
            num_scalar_prefetch=prefetch,
            grid=grid,
            in_specs=in_specs,
            out_specs=out_specs,
            scratch_shapes=list(scratch),
        ),
        compiler_params=pltpu.CompilerParams(vmem_limit_bytes=24 << 20),
    )


def near(array):
    return pltpu.with_memory_space_constraint(array, pltpu.VMEM)


def far(array):
    return pltpu.with_memory_space_constraint(array, pltpu.HBM)


def permute(array, axis, shift):
    return lax.ppermute(array, axis, ring(4, shift))


def gather_weights(block):
    z1, z3, z2 = (permute(block, "zl", r) for r in (1, 3, 2))
    a2 = permute(block, "x", 2)
    trio = jnp.concatenate([block, z1, z3], axis=0)
    g1, g3 = permute(trio, "x", 1), permute(trio, "x", 3)
    h1, h3, e2 = permute(z2, "x", 1), permute(z2, "x", 3), permute(z2, "x", 2)
    from_up, from_down = g1[1:2], g3[2:]
    f1, f3 = permute(from_up, "x", 1), permute(from_down, "x", 3)
    groups = [(a, [(dz, dx) for dz in (0, 1, 3)]) for a, dx in ((trio, 0), (g1, 1), (g3, 3))]
    groups += [(a, [(2, dx)]) for a, dx in ((z2, 0), (h1, 1), (h3, 3), (e2, 2))]
    return groups + [(a2, [(0, 2)]), (f1, [(1, 2)]), (f3, [(3, 2)])]


def step(grad_out, routes, gate, saved, w_down):
    tokens, width = grad_out.shape
    units, slots = w_down.shape[1], saved.shape[2]
    sources = slots // CAPACITY
    groups = gather_weights(w_down)
    info = jnp.stack(
        [lax.axis_index(a) for a in ("c", "zl", "x", "zh")] + [1 - lax.axis_index("zh")]
    ).astype(jnp.int32)
    half = width // 2
    blocks = half // LANES
    routes_t, gate_t = routes.T, gate.T
    keep, send = call(
        pack_kernel,
        (
            jax.ShapeDtypeStruct((tokens, half), BF16),
            jax.ShapeDtypeStruct((tokens + 16, half), BF16),
        ),
        [SMEM, VMEM, VMEM],
        (VMEM, VMEM),
    )(info, far(grad_out), far(routes_t))
    got = lax.ppermute(send, "c", ring(2, 1))
    height = CAPACITY * blocks
    peers = sources // 2

    def along_y(side, theirs, mine):
        rows = height * (theirs + mine) + 8 * mine
        array = call(
            functools.partial(dispatch_kernel, side, theirs, mine),
            jax.ShapeDtypeStruct((peers, rows, LANES), BF16),
            [SMEM] + [VMEM] * 4,
            VMEM,
        )(info, got, keep, far(routes_t), far(gate_t))
        return lax.all_to_all(array, "y", split_axis=0, concat_axis=0, tiled=True)

    def across(array):
        return lax.ppermute(array, "zh", ring(2, 1))

    cross1 = across(along_y(CROSS, True, False))
    cross2 = across(along_y(CROSS, False, True))
    stay = along_y(STAY, True, True)
    part = 512
    columns = pl.BlockSpec((slots, part), lambda j: (0, j))
    shifts = [pair for _, pairs in groups for pair in pairs]
    arrays = [a for a, _ in groups]
    product = jax.ShapeDtypeStruct((slots, units), F32)
    scratch = [pltpu.VMEM((slots, half), BF16)]
    theirs, whole = call(
        functools.partial(theirs_kernel, shifts),
        (product, jax.ShapeDtypeStruct((units, half), BF16)),
        [SMEM, VMEM, VMEM]
        + [pl.BlockSpec((a.shape[0], part, LANES), lambda j: (0, j, 0)) for a in arrays],
        (columns, VMEM),
        scratch,
        (units // part,),
    )(info, near(stay), near(cross1), *map(far, arrays))
    theirs = lax.ppermute(theirs, "c", ring(2, 1))
    mine = call(
        functools.partial(mine_kernel, shifts, height),
        product,
        [SMEM, VMEM, VMEM, VMEM],
        columns,
        scratch,
        (units // part,),
    )(info, near(stay), near(cross2), near(whole))
    steps = 4
    rows = slots // steps
    tile = (sources // steps, 8, LANES)
    wide = pl.BlockSpec((rows, 2 * units), lambda i, info: (i, 0))
    gates = pl.BlockSpec(tile, lambda i, info: (i % 2, 0, 0))
    narrow = pl.BlockSpec((rows, units), lambda i, info: (i, 0))
    plain = pl.BlockSpec((rows, units), lambda i: (i, 0))
    slopes = call(
        slopes_kernel,
        (product, product, jax.ShapeDtypeStruct((slots, units), BF16)),
        [pl.BlockSpec((rows, 2 * units), lambda i: (i, 0))],
        (plain,) * 3,
        grid=(steps,),
    )(saved[0, 0])
    grad_pre, score = call(
        finish_kernel,
        (
            jax.ShapeDtypeStruct((slots, 2 * units), BF16),
            jax.ShapeDtypeStruct((sources, 8, LANES), F32),
        ),
        [pl.BlockSpec((rows, units), lambda i, info: (piece(i, info), 0)), VMEM]
        + [narrow] * 3
        + [gates, gates],
        (wide, pl.BlockSpec(tile, lambda i, info: (i, 0, 0))),
        grid=(steps,),
        prefetch=1,
    )(info, mine, near(theirs), *slopes, stay[:, 2 * height :, :], cross2[:, height:, :])
    back = lax.all_to_all(score, EP, split_axis=0, concat_axis=0, tiled=True)
    grad_gate = call(
        home_kernel, jax.ShapeDtypeStruct((routes.shape[1], tokens), F32), [VMEM, VMEM], VMEM
    )(routes_t, back)
    return grad_pre.reshape(saved.shape), grad_gate.T


def solution(mesh):
    fine = Mesh(mesh.devices.reshape(2, 8, 4, 4, 2), ("zh", "y", "zl", "x", "c"))
    sp = ("zl", "x", "c")
    in_specs = (
        P(EP + sp, None),
        P(EP + sp, None),
        P(EP + sp, None),
        P(EP, sp, None, None),
        P(EP, None, sp),
    )
    out_specs = (P(EP, sp, None, None), P(EP + sp, None))
    return jax.shard_map(step, mesh=fine, in_specs=in_specs, out_specs=out_specs, check_vma=False)
```

```python
import functools

import jax
import jax.numpy as jnp
from jax import lax
from jax.experimental import pallas as pl
from jax.experimental.pallas import tpu as pltpu
from jax.sharding import Mesh, PartitionSpec as P


LANES = 128
CAPACITY = 16
STEP = 8
EP = ("zh", "y")
STAY, CROSS = 3, 4
F32, BF16 = jnp.float32, jnp.bfloat16
VMEM = pl.BlockSpec(memory_space=pltpu.VMEM)
SMEM = pl.BlockSpec(memory_space=pltpu.SMEM)


def ring(size, shift):
    return [((i + shift) % size, i) for i in range(size)]


def pack_kernel(core_ref, tokens_ref, routes_ref, keep_ref, send_ref):
    core = core_ref[0]
    rows = tokens_ref.shape[0]
    for ref, parity in ((keep_ref, core), (send_ref, 1 - core)):
        for b in range(ref.shape[1] // LANES):
            start = pl.multiple_of((2 * b + parity) * LANES, LANES)
            ref[:rows, b * LANES : (b + 1) * LANES] = tokens_ref[:, pl.ds(start, LANES)]
    send_ref[rows:, :] = jnp.zeros((send_ref.shape[0] - rows, send_ref.shape[1]), BF16)
    routes = routes_ref[...].astype(F32)
    send_ref[rows:, :LANES] = jnp.concatenate([routes, routes], axis=0).astype(BF16)


def places(routes, experts, first=0):
    tokens = routes.shape[1]
    wanted = (STEP * (lax.broadcasted_iota(jnp.int32, (experts, tokens), 0) + first)).astype(F32)
    hits = [routes[k : k + 1, :] == wanted for k in range(routes.shape[0])]
    member = functools.reduce(jnp.add, [h.astype(F32) for h in hits])
    before = lax.broadcasted_iota(jnp.int32, (tokens, tokens), 0) < lax.broadcasted_iota(
        jnp.int32, (tokens, tokens), 1
    )
    place = lax.dot_general(
        member.astype(BF16),
        before.astype(F32).astype(BF16),
        (((1,), (0,)), ((), ())),
        preferred_element_type=F32,
    )
    return hits, jnp.where(member > 0.5, place, -1.0)


def one_hot(place, capacity):
    experts, tokens = place.shape
    spread = jnp.broadcast_to(place[:, None, :], (experts, capacity, tokens))
    slot = lax.broadcasted_iota(jnp.int32, (experts, capacity, tokens), 1).astype(F32)
    return (spread == slot).astype(F32).reshape(experts * capacity, tokens)


def eye(shape):
    return lax.broadcasted_iota(jnp.int32, shape, 1) == lax.broadcasted_iota(jnp.int32, shape, 2)


def to_lanes(column, sources):
    rows = column.shape[0]
    shape = (sources, rows // sources, LANES)
    spread = jnp.broadcast_to(column, (rows, LANES)).reshape(shape)
    return jnp.sum(jnp.where(eye(shape), spread, 0.0), axis=1, keepdims=True)


def to_column(line, capacity):
    sources = line.shape[0]
    shape = (sources, capacity, LANES)
    spread = jnp.where(eye(shape), jnp.broadcast_to(line, shape), 0.0)
    return jnp.sum(spread.reshape(sources * capacity, LANES), axis=1, keepdims=True)


def send_rows(place, tokens_ref, out_ref, base):
    tokens = place.shape[1]
    experts, _, lanes = out_ref.shape
    chosen = one_hot(place, CAPACITY)
    rows = jnp.dot(chosen.astype(BF16), tokens_ref[:tokens, :], preferred_element_type=F32)
    rows = rows.astype(BF16)
    for b in range(rows.shape[1] // lanes):
        start = base + b * CAPACITY
        out_ref[:, start : start + CAPACITY, :] = rows[:, b * lanes : (b + 1) * lanes].reshape(
            experts, CAPACITY, lanes
        )
    return chosen


def dispatch_kernel(side, theirs, mine, info_ref, got_ref, keep_ref, routes_ref, gate_ref, out_ref):
    experts = out_ref.shape[0]
    first = info_ref[side] * experts
    height = got_ref.shape[1] // LANES * CAPACITY
    if theirs:
        table = got_ref[LANES:, :LANES].astype(F32)
        _, place = places(table[: table.shape[0] // 2], experts, first)
        send_rows(place, got_ref, out_ref, 0)
    if mine:
        base = height if theirs else 0
        gate = gate_ref[...].astype(F32)
        hits, place = places(routes_ref[...].astype(F32), experts, first)
        chosen = send_rows(place, keep_ref, out_ref, base)
        gates = functools.reduce(
            jnp.add, [jnp.where(h, gate[k : k + 1, :], 0.0) for k, h in enumerate(hits)]
        )
        spread = jnp.broadcast_to(gates[:, None, :], (experts, CAPACITY, gates.shape[1]))
        column = jnp.sum(chosen * spread.reshape(chosen.shape), axis=1, keepdims=True)
        line = to_lanes(column, experts)
        out_ref[:, base + height :, :] = jnp.broadcast_to(line, (experts, 8, LANES)).astype(BF16)


def take_rows(shifts, info_ref, sections, rows_ref):
    slots = rows_ref.shape[0] // len(sections)
    for m, (ref, base) in enumerate(sections):
        capacity = slots // ref.shape[0]
        for n, (dz, dx) in enumerate(shifts):
            chip = ((info_ref[1] + dz) & 3) * 4 + ((info_ref[2] + dx) & 3)
            start = pl.multiple_of(base + chip * capacity, capacity)
            rows_ref[m * slots : (m + 1) * slots, n * LANES : (n + 1) * LANES] = ref[
                :, pl.ds(start, capacity), :
            ].reshape(slots, LANES)


def theirs_kernel(shifts, info_ref, stay_ref, cross_ref, *refs):
    weights, (out_ref, whole_ref, rows_ref) = refs[:-3], refs[-3:]

    @pl.when(pl.program_id(0) == 0)
    def _():
        take_rows(shifts, info_ref, ((stay_ref, 0), (cross_ref, 0)), rows_ref)

    block = jnp.concatenate([w[i] for w in weights for i in range(w.shape[0])], axis=1)
    step = block.shape[0]
    whole_ref[pl.ds(pl.multiple_of(pl.program_id(0) * step, step), step), :] = block
    out_ref[...] = lax.dot_general(
        rows_ref[...], block, (((1,), (1,)), ((), ())), preferred_element_type=F32
    )


def mine_kernel(shifts, base, info_ref, stay_ref, cross_ref, whole_ref, out_ref, rows_ref):
    @pl.when(pl.program_id(0) == 0)
    def _():
        take_rows(shifts, info_ref, ((stay_ref, base), (cross_ref, 0)), rows_ref)

    step = out_ref.shape[1]
    block = whole_ref[pl.ds(pl.multiple_of(pl.program_id(0) * step, step), step), :]
    out_ref[...] = lax.dot_general(
        rows_ref[...], block, (((1,), (1,)), ((), ())), preferred_element_type=F32
    )


def piece(i, info):
    return ((i // 2) ^ info[STAY]) * 2 + i % 2


def finish_kernel(
    info_ref, mine_ref, theirs_ref, saved_ref, stay_ref, cross_ref, out_ref, score_ref
):
    rows, units = mine_ref.shape
    number = piece(pl.program_id(0), info_ref)
    here = pl.ds(pl.multiple_of(number * rows, rows), rows)
    sources = score_ref.shape[0]
    step = 256
    total = jnp.zeros((rows, LANES), F32)
    line = jnp.where(number < 2, stay_ref[...].astype(F32), cross_ref[...].astype(F32))
    gate_in = to_column(line[:, :1, :], rows // sources)
    for j in range(units // step):
        cols = slice(j * step, (j + 1) * step)
        up_cols = slice(units + j * step, units + (j + 1) * step)
        grad = mine_ref[:, cols] + theirs_ref[here, cols]
        a = saved_ref[:, cols].astype(F32)
        u = saved_ref[:, up_cols].astype(F32)
        sig = 1.0 / (1.0 + jnp.exp(-a))
        silu = a * sig
        hidden = (silu * u).astype(BF16).astype(F32)
        terms = grad * hidden
        total += terms[:, :LANES] + terms[:, LANES:]
        scaled = grad * gate_in
        out_ref[:, cols] = (scaled * u * sig * (1.0 + a * (1.0 - sig))).astype(BF16)
        out_ref[:, up_cols] = (scaled * silu).astype(BF16)
    total = jnp.sum(total, axis=1, keepdims=True)
    score_ref[...] = jnp.broadcast_to(to_lanes(total, sources), score_ref.shape)


def home_kernel(routes_ref, back_ref, out_ref):
    experts = back_ref.shape[0]
    routes = routes_ref[...].astype(F32)
    hits, place = places(routes, experts)
    chosen = one_hot(place, CAPACITY)
    column = to_column(back_ref[:, :1, :], CAPACITY)
    score = jnp.sum((column * chosen).reshape(experts, CAPACITY, -1), axis=1)
    for k, h in enumerate(hits):
        out_ref[k : k + 1, :] = jnp.sum(jnp.where(h, score, 0.0), axis=0, keepdims=True)


def call(kernel, shapes, in_specs, out_specs, scratch=(), grid=(), prefetch=0):
    return pl.pallas_call(
        kernel,
        out_shape=shapes,
        grid_spec=pltpu.PrefetchScalarGridSpec(
            num_scalar_prefetch=prefetch,
            grid=grid,
            in_specs=in_specs,
            out_specs=out_specs,
            scratch_shapes=list(scratch),
        ),
        compiler_params=pltpu.CompilerParams(vmem_limit_bytes=24 << 20),
    )


def near(array):
    return pltpu.with_memory_space_constraint(array, pltpu.VMEM)


def far(array):
    return pltpu.with_memory_space_constraint(array, pltpu.HBM)


def permute(array, axis, shift):
    return lax.ppermute(array, axis, ring(4, shift))


def gather_weights(block):
    z1, z3, z2 = (permute(block, "zl", r) for r in (1, 3, 2))
    a2 = permute(block, "x", 2)
    trio = jnp.concatenate([block, z1, z3], axis=0)
    g1, g3 = permute(trio, "x", 1), permute(trio, "x", 3)
    h1, h3, e2 = permute(z2, "x", 1), permute(z2, "x", 3), permute(z2, "x", 2)
    from_up, from_down = g1[1:2], g3[2:]
    f1, f3 = permute(from_up, "x", 1), permute(from_down, "x", 3)
    groups = [(a, [(dz, dx) for dz in (0, 1, 3)]) for a, dx in ((trio, 0), (g1, 1), (g3, 3))]
    groups += [(a, [(2, dx)]) for a, dx in ((z2, 0), (h1, 1), (h3, 3), (e2, 2))]
    return groups + [(a2, [(0, 2)]), (f1, [(1, 2)]), (f3, [(3, 2)])]


def step(grad_out, routes, gate, saved, w_down):
    tokens, width = grad_out.shape
    units, slots = w_down.shape[1], saved.shape[2]
    sources = slots // CAPACITY
    groups = gather_weights(w_down)
    info = jnp.stack(
        [lax.axis_index(a) for a in ("c", "zl", "x", "zh")] + [1 - lax.axis_index("zh")]
    ).astype(jnp.int32)
    half = width // 2
    blocks = half // LANES
    routes_t, gate_t = routes.T, gate.T
    keep, send = call(
        pack_kernel,
        (
            jax.ShapeDtypeStruct((tokens, half), BF16),
            jax.ShapeDtypeStruct((tokens + 16, half), BF16),
        ),
        [SMEM, VMEM, VMEM],
        (VMEM, VMEM),
    )(info, far(grad_out), far(routes_t))
    got = lax.ppermute(send, "c", ring(2, 1))
    height = CAPACITY * blocks
    peers = sources // 2

    def along_y(side, theirs, mine):
        rows = height * (theirs + mine) + 8 * mine
        array = call(
            functools.partial(dispatch_kernel, side, theirs, mine),
            jax.ShapeDtypeStruct((peers, rows, LANES), BF16),
            [SMEM] + [VMEM] * 4,
            VMEM,
        )(info, got, keep, far(routes_t), far(gate_t))
        return lax.all_to_all(array, "y", split_axis=0, concat_axis=0, tiled=True)

    def across(array):
        return lax.ppermute(array, "zh", ring(2, 1))

    cross1 = across(along_y(CROSS, True, False))
    cross2 = across(along_y(CROSS, False, True))
    stay = along_y(STAY, True, True)
    part = 512
    columns = pl.BlockSpec((slots, part), lambda j: (0, j))
    shifts = [pair for _, pairs in groups for pair in pairs]
    arrays = [a for a, _ in groups]
    product = jax.ShapeDtypeStruct((slots, units), F32)
    scratch = [pltpu.VMEM((slots, half), BF16)]
    theirs, whole = call(
        functools.partial(theirs_kernel, shifts),
        (product, jax.ShapeDtypeStruct((units, half), BF16)),
        [SMEM, VMEM, VMEM]
        + [pl.BlockSpec((a.shape[0], part, LANES), lambda j: (0, j, 0)) for a in arrays],
        (columns, VMEM),
        scratch,
        (units // part,),
    )(info, near(stay), near(cross1), *map(far, arrays))
    theirs = lax.ppermute(theirs, "c", ring(2, 1))
    mine = call(
        functools.partial(mine_kernel, shifts, height),
        product,
        [SMEM, VMEM, VMEM, VMEM],
        columns,
        scratch,
        (units // part,),
    )(info, near(stay), near(cross2), near(whole))
    steps = 4
    rows = slots // steps
    tile = (sources // steps, 8, LANES)
    wide = pl.BlockSpec((rows, 2 * units), lambda i, info: (i, 0))
    gates = pl.BlockSpec(tile, lambda i, info: (i % 2, 0, 0))
    grad_pre, score = call(
        finish_kernel,
        (
            jax.ShapeDtypeStruct((slots, 2 * units), BF16),
            jax.ShapeDtypeStruct((sources, 8, LANES), F32),
        ),
        [pl.BlockSpec((rows, units), lambda i, info: (piece(i, info), 0)), VMEM, wide, gates, gates],
        (wide, pl.BlockSpec(tile, lambda i, info: (i, 0, 0))),
        grid=(steps,),
        prefetch=1,
    )(info, mine, near(theirs), saved[0, 0], stay[:, 2 * height :, :], cross2[:, height:, :])
    back = lax.all_to_all(score, EP, split_axis=0, concat_axis=0, tiled=True)
    grad_gate = call(
        home_kernel, jax.ShapeDtypeStruct((routes.shape[1], tokens), F32), [VMEM, VMEM], VMEM
    )(routes_t, back)
    return grad_pre.reshape(saved.shape), grad_gate.T


def solution(mesh):
    fine = Mesh(mesh.devices.reshape(2, 8, 4, 4, 2), ("zh", "y", "zl", "x", "c"))
    sp = ("zl", "x", "c")
    in_specs = (
        P(EP + sp, None),
        P(EP + sp, None),
        P(EP + sp, None),
        P(EP, sp, None, None),
        P(EP, None, sp),
    )
    out_specs = (P(EP, sp, None, None), P(EP + sp, None))
    return jax.shard_map(step, mesh=fine, in_specs=in_specs, out_specs=out_specs, check_vma=False)
```
